256 devices in a mesh: fold: 8 (over x, core), blk: 32 (over z, y).
Axes of the slice: x: 4, y: 4, z: 8, core: 2. Of those that a mesh axis runs over, the one named last changes fastest.
Arguments:
- fine_rhs: float32 [12288, 32, 128], P(('fold', 'blk')), may hold values from -6 to 6
- fine_tiles: bfloat16 [12288, 5, 128, 128], P(('fold', 'blk')), as said below
- fine_cols: int32 [12288, 5], P(('fold', 'blk')), may hold values from 0 to 12287, as said below
- fine_smoother: bfloat16 [12288, 128, 128], P(('fold', 'blk'))
- fine_map: int32 [12288], P(('fold', 'blk')), may hold values from 0 to 3071, as said below
- fine_slots: int32 [12288, 128], P(('fold', 'blk')), may hold values from 0 to 127
- mid_tiles: bfloat16 [3072, 5, 128, 128], P(('fold', 'blk'))
- mid_cols: int32 [3072, 5], P(('fold', 'blk')), may hold values from 0 to 3071, as said below
- mid_smoother: bfloat16 [3072, 128, 128], P(('fold', 'blk'))
- mid_map: int32 [3072], P(('fold', 'blk')), may hold values from 0 to 767, as said below
- mid_slots: int32 [3072, 128], P(('fold', 'blk')), may hold values from 0 to 127
- coarse_tiles: bfloat16 [768, 5, 128, 128], P('blk')
- coarse_cols: int32 [768, 5], P('blk'), may hold values from 0 to 767, as said below
- coarse_smoother: bfloat16 [768, 128, 128], P('blk')
Outputs:
- fine_field: float32 [12288, 32, 128], P(('fold', 'blk'))
- mid_field: float32 [3072, 32, 128], P(('fold', 'blk'))
- coarse_field: float32 [768, 32, 128], P('blk')
The draws below stay inside these ranges and needn't reach their ends.
Inputs may be any that keep to these rules, and one draw needn't show every extreme that they name: `fine_cols`: column 0 of each row names the row's own block; every other entry names a level-0 block of a device with the same fold index whose blk index differs by at most one, cyclically. `mid_cols`: column 0 of each row names the row's own block; every other entry names a level-1 block of a device with the same fold index whose blk index differs by at most one, cyclically. `coarse_cols`: column 0 of each row names the row's own block; every other entry names a level-2 block whose blk index differs from the row's by at most one, cyclically. `fine_map`: A level-0 block's level-1 block lies on a device with the same fold index; of the level-0 blocks of one device at most 3 have their level-1 blocks on any one device, and in every fold row some device receives exactly 3 from every device of that row. `mid_map`: A level-1 block's level-2 block lies at the same blk index. `fine_tiles`: each smoother tile is close to half the inverse of the diagonal of the row block's diagonal tile.
All inputs are finite; a program needn't handle non-finite values.
Results may differ from the reference program's by a relative error of at most 0.012.
Values may be sent and summed in bfloat16 or wider, within the bound.
A program may use at most 128 MiB of HBM per device.

```python
import math
import jax
import jax.numpy as jnp
from jax import lax

VB = 128
R = 32
KT = 5
PRE = 2
POST = 1
COARSE = 8
B0 = 48
B1 = 12
B2 = 24
CAP = 3
NB0 = 12288
NB1 = 3072
NB2 = 768
N_FOLD = 8
N_BLK = 32


def level_diagonal(key, count):
    top_value = 2.0
    return jax.random.uniform(jax.random.fold_in(key, 11), (count, VB), jnp.float32, 1.0, top_value)


def level_tiles(key, count):
    diagonal = level_diagonal(key, count)
    spread_value = 0.03
    others = jax.random.normal(jax.random.fold_in(key, 12), (count, KT, VB, VB), jnp.float32) * spread_value
    identity = jnp.eye(VB, dtype=jnp.float32)
    leading = others[:, 0] + identity[None, :, :] * diagonal[:, :, None]
    return jnp.concatenate([leading[:, None], others[:, 1:]], axis=1)


def level_smoother(key, count):
    diagonal = level_diagonal(key, count)
    noise_part = jax.random.normal(jax.random.fold_in(key, 13), (count, VB, VB), jnp.float32) * 0.005
    identity = jnp.eye(VB, dtype=jnp.float32)
    return noise_part + identity[None, :, :] * (0.5 / diagonal)[:, :, None]


def level_columns(key, count, per_device):
    index = jnp.arange(count, dtype=jnp.int32)
    device = index // per_device
    fold_row = device // N_BLK
    blk_pos = device % N_BLK
    stepping = jax.random.randint(jax.random.fold_in(key, 21), (count, KT - 1), -1, 2)
    local_pick = jax.random.randint(jax.random.fold_in(key, 22), (count, KT - 1), 0, per_device)
    neighbour = (blk_pos[:, None] + stepping + N_BLK) % N_BLK
    others = (fold_row[:, None] * N_BLK + neighbour) * per_device + local_pick
    return jnp.concatenate([index[:, None], others], axis=1).astype(jnp.int32)


def draw_fine_tiles(key, part):
    return level_tiles(jax.random.fold_in(key, 100), NB0).astype(jnp.bfloat16)


def draw_fine_smoother(key, part):
    return level_smoother(jax.random.fold_in(key, 100), NB0).astype(jnp.bfloat16)


def draw_mid_tiles(key, part):
    return level_tiles(jax.random.fold_in(key, 200), NB1).astype(jnp.bfloat16)


def draw_mid_smoother(key, part):
    return level_smoother(jax.random.fold_in(key, 200), NB1).astype(jnp.bfloat16)


def draw_coarse_tiles(key, part):
    return level_tiles(jax.random.fold_in(key, 300), NB2).astype(jnp.bfloat16)


def draw_coarse_smoother(key, part):
    return level_smoother(jax.random.fold_in(key, 300), NB2).astype(jnp.bfloat16)


def draw_fine_cols(key, part):
    return level_columns(jax.random.fold_in(key, 110), NB0, B0)


def draw_mid_cols(key, part):
    return level_columns(jax.random.fold_in(key, 210), NB1, B1)


def draw_coarse_cols(key, part):
    return level_columns(jax.random.fold_in(key, 310), NB2, B2)


def draw_fine_map(key, part):
    base_key = jax.random.fold_in(key, 400)
    total_slots = N_BLK * CAP
    hottest = jax.random.randint(jax.random.fold_in(base_key, 1), (N_FOLD,), 0, N_BLK)

    def one_device(device):
        inner = jax.random.fold_in(base_key, device + 10)
        ordering = jax.random.permutation(jax.random.fold_in(inner, 1), total_slots)
        fold_row = device // N_BLK
        chosen = hottest[fold_row]
        scores = jnp.where(ordering // CAP == chosen, total_slots, 0) + jnp.arange(total_slots, dtype=jnp.int32)
        remaining = ordering[jnp.argsort(scores)]
        picks = jnp.concatenate([chosen * CAP + jnp.arange(CAP, dtype=jnp.int32), remaining])[:B0]
        picks = picks[jax.random.permutation(jax.random.fold_in(inner, 2), B0)]
        local_pick = jax.random.randint(jax.random.fold_in(inner, 3), (B0,), 0, B1)
        return (fold_row * N_BLK + picks // CAP) * B1 + local_pick
    mapped = jax.vmap(one_device)(jnp.arange(N_FOLD * N_BLK, dtype=jnp.int32))
    return mapped.reshape(-1).astype(jnp.int32)


def draw_mid_map(key, part):
    base_key = jax.random.fold_in(key, 500)
    index = jnp.arange(NB1, dtype=jnp.int32)
    blk_pos = index // B1 % N_BLK
    local_pick = jax.random.randint(base_key, (NB1,), 0, B2)
    return (blk_pos * B2 + local_pick).astype(jnp.int32)


def touch_ends(values, stream_key, least, high):
    spot = [jax.random.randint(jax.random.fold_in(stream_key, axis), (), 0, length) for axis, length in enumerate(values.shape)]
    longest = values.shape.index(max(values.shape))
    beside = spot[:longest] + [(spot[longest] + 1) % values.shape[longest]] + spot[longest + 1:]
    return values.at[tuple(spot)].set(least).at[tuple(beside)].set(high)


def block_levels(rng, shape, pieces, low, high):
    gain, own = 1.0, jax.random.fold_in(rng, 6)
    for position, parts in pieces:
        heights = jnp.exp(jax.random.uniform(jax.random.fold_in(own, position), (parts,), jnp.float32, low / len(pieces), high / len(pieces)))
        gain = gain * jnp.repeat(heights, shape[position] // parts).reshape([-1 if axis == position else 1 for axis in range(len(shape))])
    return gain


def gaussian(stream_key, extent, deviation, limit, cuts=(), kind=jnp.bfloat16):
    values = jax.random.normal(stream_key, extent, jnp.float32) * deviation
    if len(cuts) > 0:
        values = block_levels(stream_key, extent, cuts, -0.22, 0.18) * values
    return jnp.clip(values, min=-limit, max=limit).astype(kind)


def setup_inputs(seed: int = 0) -> dict:
    arg_keys = jax.random.split(jax.random.key(seed), 15)
    fine_rhs = gaussian(arg_keys[0], (NB0, R, VB), 1.0, 6.0, ((0, 256),), jnp.float32)
    fine_tiles = draw_fine_tiles(jax.random.fold_in(arg_keys[14], 71), 0)
    fine_cols = draw_fine_cols(jax.random.fold_in(arg_keys[14], 71), 0)
    fine_smoother = draw_fine_smoother(jax.random.fold_in(arg_keys[14], 71), 0)
    fine_map = draw_fine_map(jax.random.fold_in(arg_keys[14], 71), 0)
    fine_slots = touch_ends(jax.random.randint(arg_keys[5], (NB0, VB), 0, VB), jax.random.fold_in(arg_keys[5], 1), 0, VB - 1).astype(jnp.int32)
    mid_tiles = draw_mid_tiles(jax.random.fold_in(arg_keys[14], 71), 0)
    mid_cols = draw_mid_cols(jax.random.fold_in(arg_keys[14], 71), 0)
    mid_smoother = draw_mid_smoother(jax.random.fold_in(arg_keys[14], 71), 0)
    mid_map = draw_mid_map(jax.random.fold_in(arg_keys[14], 71), 0)
    mid_slots = touch_ends(jax.random.randint(arg_keys[10], (NB1, VB), 0, VB), jax.random.fold_in(arg_keys[10], 1), 0, VB - 1).astype(jnp.int32)
    coarse_tiles = draw_coarse_tiles(jax.random.fold_in(arg_keys[14], 71), 0)
    coarse_cols = draw_coarse_cols(jax.random.fold_in(arg_keys[14], 71), 0)
    coarse_smoother = draw_coarse_smoother(jax.random.fold_in(arg_keys[14], 71), 0)
    return {"fine_rhs": fine_rhs, "fine_tiles": fine_tiles, "fine_cols": fine_cols, "fine_smoother": fine_smoother, "fine_map": fine_map, "fine_slots": fine_slots, "mid_tiles": mid_tiles, "mid_cols": mid_cols, "mid_smoother": mid_smoother, "mid_map": mid_map, "mid_slots": mid_slots, "coarse_tiles": coarse_tiles, "coarse_cols": coarse_cols, "coarse_smoother": coarse_smoother}


def apply_level(tiles, columns, field):
    rough = field.astype(jnp.bfloat16)
    count, stored = columns.shape
    group = math.gcd(count, 64)

    def one_group(tile_pair):
        group_tiles, group_cols = tile_pair
        picked = rough[group_cols]
        return jnp.einsum("ikuw,ikrw->iru", group_tiles.astype(jnp.float32), picked.astype(jnp.float32))

    result = lax.map(one_group, (tiles.reshape(count // group, group, stored, VB, VB), columns.reshape(count // group, group, stored)))
    return result.reshape(count, R, VB)


def smooth_level(smoother, resid):
    rough = resid.astype(jnp.bfloat16)
    count = smoother.shape[0]
    group = math.gcd(count, 64)

    def one_group(tile_pair):
        group_tiles, group_resid = tile_pair
        return jnp.einsum("iuw,irw->iru", group_tiles.astype(jnp.float32), group_resid.astype(jnp.float32))

    result = lax.map(one_group, (smoother.reshape(count // group, group, VB, VB), rough.reshape(count // group, group, R, VB)))
    return result.reshape(count, R, VB)


def restrict_level(resid, coarse_map, slots, coarse_count):
    count = resid.shape[0]
    flat_rows = resid.transpose(0, 2, 1).reshape(count * VB, R)
    index = (coarse_map[:, None] * VB + slots).reshape(-1).astype(jnp.int32)
    summed = jax.ops.segment_sum(flat_rows, index, num_segments=coarse_count * VB)
    return summed.reshape(coarse_count, VB, R).transpose(0, 2, 1)


def prolong_level(coarse, coarse_map, slots):
    count = coarse_map.shape[0]
    flat_rows = coarse.transpose(0, 2, 1).reshape(-1, R)
    index = (coarse_map[:, None] * VB + slots).reshape(-1).astype(jnp.int32)
    return flat_rows[index].reshape(count, VB, R).transpose(0, 2, 1)


def smooth_sweeps(tiles, columns, smoother, rhs_field, field, sweeps):
    for sweep_turn in range(sweeps):
        field = field + smooth_level(smoother, rhs_field - apply_level(tiles, columns, field))
    return field


def reference(fine_rhs, fine_tiles, fine_cols, fine_smoother, fine_map, fine_slots, mid_tiles, mid_cols, mid_smoother, mid_map, mid_slots, coarse_tiles, coarse_cols, coarse_smoother):
    fine_pre = smooth_level(fine_smoother, fine_rhs)
    fine_pre = smooth_sweeps(fine_tiles, fine_cols, fine_smoother, fine_rhs, fine_pre, PRE - 1)
    mid_rhs = restrict_level(fine_rhs - apply_level(fine_tiles, fine_cols, fine_pre), fine_map, fine_slots, NB1)
    mid_pre = smooth_level(mid_smoother, mid_rhs)
    mid_pre = smooth_sweeps(mid_tiles, mid_cols, mid_smoother, mid_rhs, mid_pre, PRE - 1)
    coarse_rhs = restrict_level(mid_rhs - apply_level(mid_tiles, mid_cols, mid_pre), mid_map, mid_slots, NB2)
    coarse_field = smooth_level(coarse_smoother, coarse_rhs)
    coarse_field = smooth_sweeps(coarse_tiles, coarse_cols, coarse_smoother, coarse_rhs, coarse_field, COARSE - 1)
    mid_field = mid_pre + prolong_level(coarse_field, mid_map, mid_slots)
    mid_field = smooth_sweeps(mid_tiles, mid_cols, mid_smoother, mid_rhs, mid_field, POST)
    fine_field = fine_pre + prolong_level(mid_field, fine_map, fine_slots)
    fine_field = smooth_sweeps(fine_tiles, fine_cols, fine_smoother, fine_rhs, fine_field, POST)
    return (fine_field, mid_field, coarse_field)
```

```python
import functools

import jax
import jax.numpy as jnp
from jax import lax
from jax.experimental import pallas as pl
from jax.experimental.pallas import tpu as pltpu
from jax.sharding import PartitionSpec as P

COARSE = 8
CAP = 3
CHUNKS = 4
MESH = pl.DeviceIdType.MESH
F32 = jnp.float32
BF16 = jnp.bfloat16


def times(left, right):
    return lax.dot_general(
        left, right, (((1,), (1,)), ((), ())), preferred_element_type=F32
    )


def group_of(count, most):
    return max(size for size in range(1, most + 1) if count % size == 0)


def for_rows(start, count, body, most=4):
    size = group_of(count, most)

    def step(turn, carry):
        first = start + turn * size
        body([first + k for k in range(size)])
        return carry

    lax.fori_loop(0, count // size, step, 0)


def applied(tiles, cols, wide, row, stored):
    picked = jnp.concatenate(
        [wide[cols[row * stored + k]] for k in range(stored)], axis=1
    )
    tile = jnp.concatenate([tiles[row, k] for k in range(stored)], axis=1)
    return times(picked, tile)


def chosen(slots, row):
    line = slots[pl.ds(row, 1), :]
    width = line.shape[1]
    places = lax.broadcasted_iota(jnp.int32, (width, width), 0)
    return jnp.where(places == line, 1.0, 0.0).astype(BF16)


class Links:
    def __init__(self):
        self.fold = lax.axis_index("fold")
        self.blk = lax.axis_index("blk")
        self.folds = lax.axis_size("fold")
        self.blks = lax.axis_size("blk")

    def along_blk(self, step):
        return (self.fold, lax.rem(self.blk + step + self.blks, self.blks))

    def along_fold(self, step):
        return (lax.rem(self.fold + step, self.folds), self.blk)

    def greet_blk(self, barrier):
        def step(k, carry):
            pl.semaphore_signal(
                barrier, inc=1, device_id=self.along_blk(k), device_id_type=MESH
            )
            return carry

        lax.fori_loop(1, self.blks, step, 0)

    def greet_fold(self, barrier):
        def step(k, carry):
            pl.semaphore_signal(
                barrier, inc=1, device_id=self.along_fold(k), device_id_type=MESH
            )
            return carry

        lax.fori_loop(1, self.folds, step, 0)


def remote(source, target, send, recv, device):
    return pltpu.make_async_remote_copy(
        src_ref=source,
        dst_ref=target,
        send_sem=send,
        recv_sem=recv,
        device_id=device,
        device_id_type=MESH,
    )


def halo_copies(links, wide, count, first, rows, send, recv, part):
    own = wide.at[pl.ds(count + first, rows)]
    up = remote(
        own,
        wide.at[pl.ds(first, rows)],
        send.at[0, part],
        recv.at[0, part],
        links.along_blk(1),
    )
    down = remote(
        own,
        wide.at[pl.ds(2 * count + first, rows)],
        send.at[1, part],
        recv.at[1, part],
        links.along_blk(-1),
    )
    return up, down


def down_kernel(
    cols,
    sidx,
    rhs_h,
    tiles_h,
    smo_h,
    slots,
    goals,
    pre_o,
    recv_o,
    goals_o,
    rhs,
    tiles,
    smo,
    pre,
    wide0,
    wide1,
    piece,
    outbox,
    in_sem,
    pre_sem,
    own_sem,
    send0,
    recv0,
    send1,
    recv1,
    send2,
    recv2,
    send3,
    recv3,
):
    links = Links()
    count, stored = tiles.shape[0], tiles.shape[1]
    blks = links.blks
    chunk = count // CHUNKS
    loads = []
    for k, (source, target) in enumerate(((rhs_h, rhs), (smo_h, smo), (tiles_h, tiles))):
        for part in range(CHUNKS):
            rows = pl.ds(part * chunk, chunk)
            loads.append(
                pltpu.make_async_copy(
                    source.at[rows], target.at[rows], in_sem.at[k, part]
                )
            )
    for part in range(CHUNKS):
        loads[part].start()
        loads[CHUNKS + part].start()
    for part in range(CHUNKS):
        loads[2 * CHUNKS + part].start()
    barrier = pltpu.get_barrier_semaphore()
    links.greet_blk(barrier)

    def goal_copy(k):
        return remote(
            goals.at[k],
            goals_o.at[k],
            send3.at[k],
            recv3.at[k],
            links.along_blk(k),
        )

    def piece_copy(k):
        return remote(
            outbox.at[k],
            recv_o.at[k],
            send2.at[k],
            recv2.at[k],
            links.along_blk(k),
        )

    own_goals = pltpu.make_async_copy(goals.at[0], goals_o.at[0], own_sem.at[0])
    own_piece = pltpu.make_async_copy(outbox.at[0], recv_o.at[0], own_sem.at[1])
    own_goals.start()

    halos0, halos1 = [], []
    for part in range(CHUNKS):
        loads[part].wait()
        loads[CHUNKS + part].wait()

        def first_rows(rows):
            fresh = [times(rhs[i].astype(BF16), smo[i]) for i in rows]
            for i, z in zip(rows, fresh):
                pre[i] = z
                wide0[count + i] = z.astype(BF16)

        for_rows(part * chunk, chunk, first_rows)
        if part == 0:
            pl.semaphore_wait(barrier, blks - 1)
        for copy in halo_copies(
            links, wide0, count, part * chunk, chunk, send0, recv0, part
        ):
            copy.start()
            halos0.append(copy)

    for part in range(CHUNKS):
        loads[2 * CHUNKS + part].wait()
    for copy in halos0:
        copy.wait_recv()

    for part in range(CHUNKS):

        def sweep_rows(rows):
            resid = [
                (rhs[i] - applied(tiles, cols, wide0, i, stored)).astype(BF16)
                for i in rows
            ]
            fresh = [pre[i] + times(g, smo[i]) for i, g in zip(rows, resid)]
            for i, z in zip(rows, fresh):
                pre[i] = z
                wide1[count + i] = z.astype(BF16)

        for_rows(part * chunk, chunk, sweep_rows)
        for copy in halo_copies(
            links, wide1, count, part * chunk, chunk, send1, recv1, part
        ):
            copy.start()
            halos1.append(copy)
    keep = pltpu.make_async_copy(pre, pre_o, pre_sem)
    keep.start()

    def goal_step(k, carry):
        goal_copy(k).start()
        return carry

    lax.fori_loop(1, blks, goal_step, 0)
    for copy in halos1:
        copy.wait_recv()

    def piece_rows(rows):
        resid = [
            (rhs[i] - applied(tiles, cols, wide1, i, stored)).astype(BF16)
            for i in rows
        ]
        sums = [times(g, chosen(slots, i)) for i, g in zip(rows, resid)]
        for i, z in zip(rows, sums):
            piece[i] = z.astype(BF16)

    for_rows(0, count, piece_rows)

    def pack(k):
        for s in range(CAP):
            outbox[k, s] = piece[sidx[k * CAP + s]]

    def send_step(k, carry):
        pack(k)
        piece_copy(k).start()
        return carry

    lax.fori_loop(1, blks, send_step, 0)
    pack(0)
    own_piece.start()
    for copy in halos0 + halos1:
        copy.wait_send()

    def end_step(k, carry):
        goal_copy(k).wait()
        piece_copy(k).wait()
        return carry

    lax.fori_loop(1, blks, end_step, 0)
    own_goals.wait()
    own_piece.wait()
    keep.wait()


def up_kernel(
    goals,
    mcols,
    ccols,
    low,
    places,
    fcols,
    recv_h,
    mtiles_h,
    msmo_h,
    mslots,
    ctiles_h,
    csmo_h,
    rhs_h,
    pre_h,
    tiles_h,
    smo_h,
    slots,
    fine_o,
    mid_o,
    coarse_o,
    inbox,
    mtiles,
    msmo,
    ctiles,
    csmo,
    rhs,
    pre,
    tiles,
    smo,
    mrhs,
    mpre,
    mpiece,
    mwide,
    mfield,
    mround,
    parts,
    fold_send,
    fold_recv,
    crhs,
    cfield,
    cwide,
    gathered,
    coarse,
    outbox,
    backbox,
    fwide,
    in_sem,
    out_sem,
    msend,
    mrecv,
    rsend,
    rrecv,
    csend,
    crecv,
    gsend,
    grecv,
    bsend,
    brecv,
    fsend,
    frecv,
):
    links = Links()
    folds, blks = links.folds, links.blks
    count, stored = tiles.shape[0], tiles.shape[1]
    mcount = mtiles.shape[0]
    half = ctiles.shape[0]
    wide_r = crhs.shape[1]
    groups = folds // 2
    core = lax.rem(links.fold, 2)
    group = links.fold // 2
    sources = (
        (recv_h, inbox),
        (msmo_h, msmo),
        (mtiles_h, mtiles),
        (csmo_h.at[pl.ds(core * half, half)], csmo),
        (ctiles_h.at[pl.ds(core * half, half)], ctiles),
        (rhs_h, rhs),
        (pre_h, pre),
        (tiles_h, tiles),
        (smo_h, smo),
    )
    loads = [
        pltpu.make_async_copy(source, target, in_sem.at[k])
        for k, (source, target) in enumerate(sources)
    ]
    for load in loads:
        load.start()
    barrier = pltpu.get_barrier_semaphore()
    links.greet_blk(barrier)
    links.greet_fold(barrier)

    loads[0].wait()
    zero = jnp.zeros(mrhs.shape[1:], F32)
    tied = group_of(mcount, 12)
    for first in range(0, mcount, tied):

        def add_piece(p, sums):
            src, s = p // CAP, lax.rem(p, CAP)
            value = inbox[src, s].astype(F32)
            goal = goals[src, 0, s]
            return tuple(
                total + jnp.where(goal == first + t, value, zero)
                for t, total in enumerate(sums)
            )

        sums = lax.fori_loop(0, blks * CAP, add_piece, (zero,) * tied)
        for t, total in enumerate(sums):
            mrhs[first + t] = total
    loads[1].wait()

    def mid_first(rows):
        fresh = [times(mrhs[i].astype(BF16), msmo[i]) for i in rows]
        for i, z in zip(rows, fresh):
            mpre[i] = z
            mwide[0][mcount + i] = z.astype(BF16)

    for_rows(0, mcount, mid_first)
    pl.semaphore_wait(barrier, blks - 1 + folds - 1)

    def mid_halo(k):
        return halo_copies(
            links, mwide[k], mcount, 0, mcount, msend.at[k], mrecv.at[k], 0
        )

    def start_halo(copies):
        for copy in copies:
            copy.start()

    def end_halo(copies):
        for copy in copies:
            copy.wait()

    start_halo(mid_halo(0))
    loads[2].wait()
    end_halo(mid_halo(0))

    def mid_sweep(rows):
        resid = [
            (mrhs[i] - applied(mtiles, mcols, mwide[0], i, stored)).astype(BF16)
            for i in rows
        ]
        fresh = [mpre[i] + times(g, msmo[i]) for i, g in zip(rows, resid)]
        for i, z in zip(rows, fresh):
            mpre[i] = z
            mwide[1][mcount + i] = z.astype(BF16)

    for_rows(0, mcount, mid_sweep)
    start_halo(mid_halo(1))
    end_halo(mid_halo(1))

    def mid_pieces(rows):
        resid = [
            (mrhs[i] - applied(mtiles, mcols, mwide[1], i, stored)).astype(BF16)
            for i in rows
        ]
        sums = [times(g, chosen(mslots, i)) for i, g in zip(rows, resid)]
        for i, z in zip(rows, sums):
            mpiece[i] = z

    for_rows(0, mcount, mid_pieces)

    def low_terms(c, carry):
        total = zero
        for j in range(mcount):
            total = total + jnp.where(low[j] == c, mpiece[j], zero)
        place = c // half
        row = lax.rem(c, half)
        for g in range(groups):
            parts[2 * g + place, row] = total[g * wide_r : (g + 1) * wide_r]
        return carry

    lax.fori_loop(0, 2 * half, low_terms, 0)
    fold_send[...] = parts[...].astype(BF16)

    def fold_copy(k):
        to = links.along_fold(k)
        return remote(
            fold_send.at[to[0]], fold_recv.at[k], rsend.at[k], rrecv.at[k], to
        )

    for k in range(1, folds):
        fold_copy(k).start()
    fold_recv[0] = fold_send[links.fold]
    loads[3].wait()
    loads[4].wait()
    for k in range(1, folds):
        fold_copy(k).wait()
    total = fold_recv[0].astype(F32)
    for k in range(1, folds):
        total = total + fold_recv[k].astype(F32)
    crhs[...] = total

    mine = 2 * half + core * half

    def coarse_copies(k):
        own = cwide[k].at[pl.ds(mine, half)]
        other = links.fold + 1 - 2 * core
        copies = []
        place = 0
        for step, offset in ((0, 1), (1, 0), (-1, 2)):
            blk = lax.rem(links.blk + step + blks, blks)
            for fold in (other,) if step == 0 else (links.fold, other):
                copies.append(
                    remote(
                        own,
                        cwide[k].at[pl.ds(offset * 2 * half + core * half, half)],
                        csend.at[k, place],
                        crecv.at[k, place],
                        (fold, blk),
                    )
                )
                place += 1
        return copies

    def coarse_first(rows):
        fresh = [times(crhs[i].astype(BF16), csmo[i]) for i in rows]
        for i, z in zip(rows, fresh):
            cfield[i] = z
            cwide[0][mine + i] = z.astype(BF16)

    for_rows(0, half, coarse_first)

    for k in range(COARSE - 1):
        start_halo(coarse_copies(k))
        end_halo(coarse_copies(k))

        def coarse_sweep(rows):
            resid = [
                (crhs[i] - applied(ctiles, ccols, cwide[k], i, stored)).astype(BF16)
                for i in rows
            ]
            fresh = [cfield[i] + times(g, csmo[i]) for i, g in zip(rows, resid)]
            for i, z in zip(rows, fresh):
                cfield[i] = z
                cwide[k + 1][mine + i] = z.astype(BF16)

        for_rows(0, half, coarse_sweep)

    def gather_copy(k):
        return remote(
            cwide[COARSE - 1].at[pl.ds(mine, half)],
            gathered.at[links.fold],
            gsend.at[k],
            grecv.at[k],
            links.along_fold(k),
        )

    for k in range(1, folds):
        gather_copy(k).start()
    gathered[links.fold] = cwide[COARSE - 1][pl.ds(mine, half)]
    for k in range(1, folds):
        gather_copy(k).wait()
    for f in range(folds):
        g, place = f // 2, f % 2
        coarse[pl.ds(place * half, half), pl.ds(g * wide_r, wide_r), :] = gathered[
            f
        ].astype(F32)
    keep_coarse = pltpu.make_async_copy(coarse, coarse_o, out_sem.at[0])
    keep_coarse.start()

    def mid_lift(rows):
        lifted = [
            jnp.dot(
                coarse[low[i]].astype(BF16),
                chosen(mslots, i),
                preferred_element_type=F32,
            )
            for i in rows
        ]
        fresh = [mpre[i] + z for i, z in zip(rows, lifted)]
        for i, z in zip(rows, fresh):
            mpre[i] = z
            mwide[2][mcount + i] = z.astype(BF16)

    for_rows(0, mcount, mid_lift)
    start_halo(mid_halo(2))
    end_halo(mid_halo(2))

    def mid_last(rows):
        resid = [
            (mrhs[i] - applied(mtiles, mcols, mwide[2], i, stored)).astype(BF16)
            for i in rows
        ]
        fresh = [mpre[i] + times(g, msmo[i]) for i, g in zip(rows, resid)]
        for i, z in zip(rows, fresh):
            mfield[i] = z
            mround[i] = z.astype(BF16)

    for_rows(0, mcount, mid_last)
    keep_mid = pltpu.make_async_copy(mfield, mid_o, out_sem.at[1])
    keep_mid.start()


    def back_copy(k):
        return remote(
            outbox.at[k],
            backbox.at[pl.ds(k * CAP, CAP)],
            bsend.at[k],
            brecv.at[k],
            links.along_blk(k),
        )

    def back_step(k, carry):
        back = lax.rem(blks - k, blks)
        for s in range(CAP):
            outbox[k, s] = mround[jnp.minimum(goals[back, 0, s], mcount - 1)]
        back_copy(k).start()
        return carry

    lax.fori_loop(1, blks, back_step, 0)
    for s in range(CAP):
        backbox[s] = mround[jnp.minimum(goals[0, 0, s], mcount - 1)]
    for k in (5, 6, 7, 8):
        loads[k].wait()

    def back_end(k, carry):
        back_copy(k).wait()
        return carry

    lax.fori_loop(1, blks, back_end, 0)

    chunk = count // CHUNKS
    halos = []
    for part in range(CHUNKS):

        def fine_lift(rows):
            lifted = [
                jnp.dot(
                    backbox[places[i]], chosen(slots, i), preferred_element_type=F32
                )
                for i in rows
            ]
            fresh = [pre[i] + z for i, z in zip(rows, lifted)]
            for i, z in zip(rows, fresh):
                pre[i] = z
                fwide[count + i] = z.astype(BF16)

        for_rows(part * chunk, chunk, fine_lift)
        for copy in halo_copies(
            links, fwide, count, part * chunk, chunk, fsend, frecv, part
        ):
            copy.start()
            halos.append(copy)
    for copy in halos:
        copy.wait()
    keeps = []
    for part in range(CHUNKS):

        def fine_last(rows):
            resid = [
                (rhs[i] - applied(tiles, fcols, fwide, i, stored)).astype(BF16)
                for i in rows
            ]
            fresh = [pre[i] + times(g, smo[i]) for i, g in zip(rows, resid)]
            for i, z in zip(rows, fresh):
                pre[i] = z

        for_rows(part * chunk, chunk, fine_last)
        rows = pl.ds(part * chunk, chunk)
        keeps.append(
            pltpu.make_async_copy(pre.at[rows], fine_o.at[rows], out_sem.at[2 + part])
        )
        keeps[-1].start()
    for copy in [keep_coarse, keep_mid] + keeps:
        copy.wait()


def local_columns(columns, per_device):
    blks = lax.axis_size("blk")
    owner = columns // per_device % blks
    offset = (owner - lax.axis_index("blk") + 1 + blks) % blks
    return (offset * per_device + columns % per_device).reshape(-1)


ANY = pl.BlockSpec(memory_space=pl.ANY)
SMEM = pl.BlockSpec(memory_space=pltpu.SMEM)
VMEM = pl.BlockSpec(memory_space=pltpu.VMEM)


def on_device(
    fine_rhs,
    fine_tiles,
    fine_cols,
    fine_smoother,
    fine_map,
    fine_slots,
    mid_tiles,
    mid_cols,
    mid_smoother,
    mid_map,
    mid_slots,
    coarse_tiles,
    coarse_cols,
    coarse_smoother,
):
    count, stored, width, _ = fine_tiles.shape
    mcount = mid_tiles.shape[0]
    lcount = coarse_tiles.shape[0]
    r = fine_rhs.shape[1]
    folds, blks = lax.axis_size("fold"), lax.axis_size("blk")
    half = lcount // 2
    wide_r = r * 2 // folds
    block = (r, width)

    owner = fine_map // mcount % blks
    steps = (owner - lax.axis_index("blk") + blks) % blks
    order = jnp.arange(count, dtype=jnp.int32)
    same = (steps[:, None] == steps[None, :]) & (order[None, :] < order[:, None])
    rank = jnp.sum(same.astype(jnp.int32), axis=1)
    position = steps * CAP + rank
    hit = position[None, :] == jnp.arange(blks * CAP, dtype=jnp.int32)[:, None]
    sidx = jnp.sum(jnp.where(hit, order[None, :], 0), axis=1)
    goal = jnp.sum(jnp.where(hit, (fine_map % mcount)[None, :] - mcount, 0), axis=1) + mcount
    goals = jnp.pad(goal.reshape(blks, 1, CAP), ((0, 0), (0, 0), (0, 128 - CAP)))
    places = (blks - steps) % blks * CAP + rank
    fcols = local_columns(fine_cols, count)

    dma = pltpu.SemaphoreType.DMA
    pre, received, goals_in = pl.pallas_call(
        down_kernel,
        out_shape=(
            jax.ShapeDtypeStruct((count,) + block, F32),
            jax.ShapeDtypeStruct((blks, CAP) + block, BF16),
            jax.ShapeDtypeStruct((blks, 1, 128), jnp.int32),
        ),
        in_specs=[SMEM, SMEM, ANY, ANY, ANY, VMEM, VMEM],
        out_specs=(ANY, ANY, ANY),
        scratch_shapes=[
            pltpu.VMEM((count,) + block, F32),
            pltpu.VMEM((count, stored, width, width), BF16),
            pltpu.VMEM((count, width, width), BF16),
            pltpu.VMEM((count,) + block, F32),
            pltpu.VMEM((3 * count,) + block, BF16),
            pltpu.VMEM((3 * count,) + block, BF16),
            pltpu.VMEM((count,) + block, BF16),
            pltpu.VMEM((blks, CAP) + block, BF16),
            dma((3, CHUNKS)),
            dma(()),
            dma((2,)),
        ]
        + [dma((2, CHUNKS))] * 4
        + [dma((blks,))] * 4,
        compiler_params=pltpu.CompilerParams(
            collective_id=1, has_side_effects=True, vmem_limit_bytes=40 << 20
        ),
        name="fine_down",
    )(fcols, sidx, fine_rhs, fine_tiles, fine_smoother, fine_slots, goals)

    fine, mid, coarse = pl.pallas_call(
        up_kernel,
        out_shape=(
            jax.ShapeDtypeStruct((count,) + block, F32),
            jax.ShapeDtypeStruct((mcount,) + block, F32),
            jax.ShapeDtypeStruct((lcount,) + block, F32),
        ),
        in_specs=[SMEM] * 6 + [ANY] * 3 + [VMEM] + [ANY] * 6 + [VMEM],
        out_specs=(ANY, ANY, ANY),
        scratch_shapes=[
            pltpu.VMEM((blks, CAP) + block, BF16),
            pltpu.VMEM((mcount, stored, width, width), BF16),
            pltpu.VMEM((mcount, width, width), BF16),
            pltpu.VMEM((half, stored, width, width), BF16),
            pltpu.VMEM((half, width, width), BF16),
            pltpu.VMEM((count,) + block, F32),
            pltpu.VMEM((count,) + block, F32),
            pltpu.VMEM((count, stored, width, width), BF16),
            pltpu.VMEM((count, width, width), BF16),
            pltpu.VMEM((mcount,) + block, F32),
            pltpu.VMEM((mcount,) + block, F32),
            pltpu.VMEM((mcount,) + block, F32),
            [pltpu.VMEM((3 * mcount,) + block, BF16)] * 3,
            pltpu.VMEM((mcount,) + block, F32),
            pltpu.VMEM((mcount,) + block, BF16),
            pltpu.VMEM((folds, half, wide_r, width), F32),
            pltpu.VMEM((folds, half, wide_r, width), BF16),
            pltpu.VMEM((folds, half, wide_r, width), BF16),
            pltpu.VMEM((half, wide_r, width), F32),
            pltpu.VMEM((half, wide_r, width), F32),
            [pltpu.VMEM((3 * lcount, wide_r, width), BF16)] * COARSE,
            pltpu.VMEM((folds, half, wide_r, width), BF16),
            pltpu.VMEM((lcount,) + block, F32),
            pltpu.VMEM((blks, CAP) + block, BF16),
            pltpu.VMEM((blks * CAP,) + block, BF16),
            pltpu.VMEM((3 * count,) + block, BF16),
            dma((9,)),
            dma((2 + CHUNKS,)),
            dma((3, 2, 1)),
            dma((3, 2, 1)),
            dma((folds,)),
            dma((folds,)),
            dma((COARSE - 1, 5)),
            dma((COARSE - 1, 5)),
            dma((folds,)),
            dma((folds,)),
            dma((blks,)),
            dma((blks,)),
            dma((2, CHUNKS)),
            dma((2, CHUNKS)),
        ],
        compiler_params=pltpu.CompilerParams(
            collective_id=2, has_side_effects=True, vmem_limit_bytes=48 << 20
        ),
        name="coarse_and_up",
    )(
        goals_in,
        local_columns(mid_cols, mcount),
        local_columns(coarse_cols, lcount)
        .reshape(2, half * stored)[lax.axis_index("fold") % 2],
        mid_map % lcount,
        places,
        fcols,
        received,
        mid_tiles,
        mid_smoother,
        mid_slots,
        coarse_tiles,
        coarse_smoother,
        fine_rhs,
        pre,
        fine_tiles,
        fine_smoother,
        fine_slots,
    )
    return fine, mid, coarse


def solution(mesh):
    both = ("fold", "blk")
    placed = (
        P(both, None, None),
        P(both, None, None, None),
        P(both, None),
        P(both, None, None),
        P(both),
        P(both, None),
        P(both, None, None, None),
        P(both, None),
        P(both, None, None),
        P(both),
        P(both, None),
        P("blk", None, None, None),
        P("blk", None),
        P("blk", None, None),
    )
    return jax.shard_map(
        on_device,
        mesh=mesh,
        in_specs=placed,
        out_specs=(P(both, None, None), P(both, None, None), P("blk", None, None)),
        check_vma=False,
    )
```

```python
import jax
import jax.numpy as jnp
from jax import lax
from jax.experimental import pallas as pl
from jax.experimental.pallas import tpu as pltpu
from jax.sharding import PartitionSpec as P

COARSE = 8
CAP = 3
HALVES = 2
PARTS = 2
SPLIT = 2
SLOTS = 8
MESH = pl.DeviceIdType.MESH
F32 = jnp.float32
BF16 = jnp.bfloat16
I32 = jnp.int32


def times(left, right):
    return lax.dot_general(
        left, right, (((1,), (1,)), ((), ())), preferred_element_type=F32
    )


def group_of(count, most):
    return max(size for size in range(1, most + 1) if count % size == 0)


def for_rows(start, count, body, most=12):
    size = group_of(count, most)

    def step(turn, carry):
        first = start + turn * size
        body([first + k for k in range(size)])
        return carry

    lax.fori_loop(0, count // size, step, 0)


def each(first, last, body):
    def step(k, carry):
        body(k)
        return carry

    lax.fori_loop(first, last, step, 0)


def chosen(slots, row):
    line = slots[pl.ds(row, 1), :]
    width = line.shape[1]
    places = lax.broadcasted_iota(I32, (width, width), 0)
    return jnp.where(places == line, 1.0, 0.0).astype(BF16)


def remote(source, target, send, recv, device):
    return pltpu.make_async_remote_copy(
        src_ref=source,
        dst_ref=target,
        send_sem=send,
        recv_sem=recv,
        device_id=device,
        device_id_type=MESH,
    )


def within(index, size):
    return jnp.minimum(jnp.maximum(index, 0), size - 1)


class Level:
    def __init__(self, tiles, cols, first, span, start=0):
        self.tiles, self.cols, self.start = tiles, cols, start
        self.first, self.span = first, span

    def own(self, row, value):
        return times(value, self.tiles[row, 0])

    def others(self, row, wide):
        stored = self.tiles.shape[1]
        picked = []
        for k in range(1, stored):
            at = self.cols[k, self.start + row] - self.first
            at = jnp.where(at < 0, at + self.span, at)
            at = jnp.where(at >= self.span, at - self.span, at)
            picked.append(wide[within(at, wide.shape[0])])
        tile = jnp.concatenate([self.tiles[row, k] for k in range(1, stored)], axis=1)
        return times(jnp.concatenate(picked, axis=1), tile)


def cycle(
    fcols,
    mcols,
    ccols,
    low,
    fmap,
    slots,
    mslots,
    rhs_h,
    tiles_h,
    smo_h,
    mtiles_h,
    msmo_h,
    ctiles_h,
    csmo_h,
    fine_o,
    mid_o,
    coarse_o,
    v,
    w,
    q,
):
    fold, blk = lax.axis_index("fold"), lax.axis_index("blk")
    folds, blks = lax.axis_size("fold"), lax.axis_size("blk")
    tiles, smo, rhs, pre = v["tiles"], v["smo"], v["rhs"], v["pre"]
    mtiles, msmo, mrhs, mpre = v["mtiles"], v["msmo"], v["mrhs"], v["mpre"]
    ctiles, csmo, crhs, cfield = v["ctiles"], v["csmo"], v["crhs"], v["cfield"]
    count, mcount, half = tiles.shape[0], mtiles.shape[0], ctiles.shape[0]
    rh = rhs.shape[1] // HALVES
    chunk = count // PARTS
    wide_r = crhs.shape[1]
    groups = folds // 2
    core = lax.rem(fold, 2)
    sent = []

    def along_blk(step):
        return (fold, lax.rem(blk + step + blks, blks))

    def along_fold(step):
        return (lax.rem(fold + step, folds), blk)

    def load(source, target, place, start=0, rows=None):
        if rows is not None:
            source, target = source.at[pl.ds(start, rows)], target.at[pl.ds(start, rows)]
        return pltpu.make_async_copy(source, target, q["load"].at[place])

    first_loads = []
    for part in range(PARTS):
        first_loads.append(load(rhs_h, rhs, 2 * part, part * chunk, chunk))
        first_loads.append(load(smo_h, smo, 2 * part + 1, part * chunk, chunk))
    tile_load = load(tiles_h, tiles, 2 * PARTS)
    later = [
        load(msmo_h, msmo, 2 * PARTS + 1),
        load(mtiles_h, mtiles, 2 * PARTS + 2),
        load(csmo_h.at[pl.ds(core * half, half)], csmo, 2 * PARTS + 3),
        load(ctiles_h.at[pl.ds(core * half, half)], ctiles, 2 * PARTS + 4),
    ]
    for copy in first_loads + [tile_load]:
        copy.start()

    barrier = pltpu.get_barrier_semaphore()

    def greet(device):
        pl.semaphore_signal(barrier, inc=1, device_id=device, device_id_type=MESH)

    each(1, blks, lambda k: greet(along_blk(k)))
    each(1, folds, lambda k: greet(along_fold(k)))

    fine = Level(tiles, fcols, (fold * blks + blk - 1) * count, blks * count)
    mid = Level(mtiles, mcols, (fold * blks + blk - 1) * mcount, blks * mcount)
    low_level = Level(
        ctiles, ccols, (blk - 1) * 2 * half, blks * 2 * half, core * half
    )

    def halo(wide, size, start, rows, sems, place):
        own = wide.at[pl.ds(size + start, rows)]
        return [
            remote(
                own,
                wide.at[pl.ds(at + start, rows)],
                q[sems + "_send"].at[place, side],
                q[sems + "_recv"].at[place, side],
                along_blk(step),
            )
            for side, (at, step) in enumerate(((0, 1), (2 * size, -1)))
        ]

    def send(copies):
        for copy in copies:
            copy.start()
        sent.extend(copies)

    def received(copies):
        for copy in copies:
            copy.wait_recv()

    def fine_halo(turn, h, part):
        place = (turn * HALVES + h) * PARTS + part
        return halo(w["wide"][turn * HALVES + h], count, part * chunk, chunk, "halo", place)

    def fine_wide(turn, h):
        return w["wide"][turn * HALVES + h]

    def fine_received(turn, h):
        for part in range(PARTS):
            received(fine_halo(turn, h, part))

    def part_of_r(h):
        return pl.ds(h * rh, rh)

    for part in range(PARTS):
        first_loads[2 * part].wait()
        first_loads[2 * part + 1].wait()

        def first_rows(rows):
            fresh = [times(rhs[i].astype(BF16), smo[i]) for i in rows]
            for i, z in zip(rows, fresh):
                pre[i] = z
                for h in range(HALVES):
                    fine_wide(0, h)[count + i] = z[h * rh : (h + 1) * rh].astype(BF16)

        for_rows(part * chunk, chunk, first_rows)
        if part == 0:
            pl.semaphore_wait(barrier, blks - 1 + folds - 1)
        send(fine_halo(0, 0, part))
    for h in range(1, HALVES):
        for part in range(PARTS):
            send(fine_halo(0, h, part))
    for copy in later:
        copy.start()

    line = fmap[...] - fold * blks * mcount
    owner = lax.shift_right_logical(line * (-(-(1 << 19) // mcount)), 19)
    target = line - owner * mcount
    steps = owner - blk
    steps = jnp.where(steps < 0, steps + blks, steps)
    across = lax.broadcasted_iota(I32, (count, count), 1)
    down = lax.broadcasted_iota(I32, (count, count), 0)
    steps_down = jnp.sum(jnp.where(across == down, steps, 0), axis=1, keepdims=True)
    ahead = (steps_down == steps) & (down < across)
    rank = jnp.sum(jnp.where(ahead, 1, 0), axis=0, keepdims=True)
    position = steps * SLOTS + rank
    hit = lax.broadcasted_iota(I32, (blks * SLOTS, count), 0) == position
    order = lax.broadcasted_iota(I32, (blks * SLOTS, count), 1)
    index = jnp.sum(jnp.where(hit, order, 0), axis=1, keepdims=True)
    goal = jnp.sum(jnp.where(hit, target - mcount, 0), axis=1, keepdims=True) + mcount
    lane = lax.broadcasted_iota(I32, (blks * SLOTS, 128), 1)
    table = jnp.where(lane == 0, goal, index)
    v["table"][...] = table.reshape(blks, SLOTS, 128)
    back_steps = jnp.where(steps == 0, 0, blks - steps)
    v["places"][pl.ds(0, 1), pl.ds(0, count)] = back_steps * CAP + rank

    def small(source, target, place):
        return pltpu.make_async_copy(source, target, q["small"].at[place])

    own_table = small(v["table"], v["table_s"], 0)
    own_places = small(v["places"], v["places_s"], 1)
    own_table.start()
    own_places.start()

    def goal_copy(k):
        return remote(
            v["table"].at[k],
            v["goals"].at[k],
            q["goal_send"].at[k],
            q["goal_recv"].at[k],
            along_blk(k),
        )

    each(1, blks, lambda k: goal_copy(k).start())
    v["goals"][0] = v["table"][0]

    def fine_own(turn, h):
        def rows_of(rows):
            fresh = [
                rhs[i, part_of_r(h), :] - fine.own(i, fine_wide(turn, h)[count + i])
                for i in rows
            ]
            for i, z in zip(rows, fresh):
                w["base"][h][i] = z

        for_rows(0, count, rows_of)

    def fine_resid(turn, h, i):
        return (w["base"][h][i] - fine.others(i, fine_wide(turn, h))).astype(BF16)

    tile_load.wait()
    for h in range(HALVES):
        fine_own(0, h)

    for h in range(HALVES):
        fine_received(0, h)
        for part in range(PARTS):

            def sweep_rows(rows):
                resid = [fine_resid(0, h, i) for i in rows]
                fresh = [
                    pre[i, part_of_r(h), :] + times(g, smo[i])
                    for i, g in zip(rows, resid)
                ]
                for i, z in zip(rows, fresh):
                    pre[i, part_of_r(h), :] = z
                    fine_wide(1, h)[count + i] = z.astype(BF16)

            for_rows(part * chunk, chunk, sweep_rows)
            send(fine_halo(1, h, part))
    for h in range(HALVES):
        fine_own(1, h)
    own_table.wait()
    own_places.wait()

    def piece_copy(h, k):
        return remote(
            w["outbox"][h].at[k],
            w["inbox"][h].at[k],
            q["piece_send"].at[h, k],
            q["piece_recv"].at[h, k],
            along_blk(k),
        )

    for h in range(HALVES):
        fine_received(1, h)
        piece = w["piece"][h]

        def piece_rows(rows):
            resid = [fine_resid(1, h, i) for i in rows]
            sums = [times(g, chosen(slots, i)) for i, g in zip(rows, resid)]
            for i, z in zip(rows, sums):
                piece[i] = z.astype(BF16)

        for_rows(0, count, piece_rows)

        def pack(k):
            for s in range(CAP):
                w["outbox"][h][k, s] = piece[within(v["table_s"][k, s, 1], count)]
            piece_copy(h, k).start()

        each(1, blks, pack)
        for s in range(CAP):
            w["inbox"][h][0, s] = piece[within(v["table_s"][0, s, 1], count)]

    each(1, blks, lambda k: goal_copy(k).wait_recv())
    goals_move = small(v["goals"], v["goals_s"], 2)
    goals_move.start()
    goals_move.wait()
    goals = v["goals_s"]

    zero = jnp.zeros((rh, rhs.shape[2]), F32)
    tied = group_of(mcount, 12)
    for h in range(HALVES):
        each(1, blks, lambda k: piece_copy(h, k).wait_recv())
        for first in range(0, mcount, tied):

            def add_pieces(k, sums):
                for s in range(CAP):
                    value = w["inbox"][h][k, s].astype(F32)
                    place = goals[k, s, 0]
                    sums = tuple(
                        total + jnp.where(place == first + t, value, zero)
                        for t, total in enumerate(sums)
                    )
                return sums

            sums = lax.fori_loop(0, blks, add_pieces, (zero,) * tied)
            for t, total in enumerate(sums):
                mrhs[first + t, part_of_r(h), :] = total
    for copy in later[:2]:
        copy.wait()

    def mid_put(turn, rows, fresh):
        for i, z in zip(rows, fresh):
            mpre[i] = z
            w["mwide"][turn][mcount + i] = z.astype(BF16)

    def mid_first(rows):
        mid_put(0, rows, [times(mrhs[i].astype(BF16), msmo[i]) for i in rows])

    def mid_exchange(turn):
        wide = w["mwide"][turn]
        copies = halo(wide, mcount, 0, mcount, "mid", turn)
        send(copies)

        def own_rows(rows):
            fresh = [mrhs[i] - mid.own(i, wide[mcount + i]) for i in rows]
            for i, z in zip(rows, fresh):
                v["mbase"][i] = z

        for_rows(0, mcount, own_rows)
        received(copies)

    def mid_resid(turn, i):
        return (v["mbase"][i] - mid.others(i, w["mwide"][turn])).astype(BF16)

    for_rows(0, mcount, mid_first)
    mid_exchange(0)

    def mid_sweep(rows):
        resid = [mid_resid(0, i) for i in rows]
        mid_put(1, rows, [mpre[i] + times(g, msmo[i]) for i, g in zip(rows, resid)])

    for_rows(0, mcount, mid_sweep)
    mid_exchange(1)

    def mid_pieces(rows):
        resid = [mid_resid(1, i) for i in rows]
        sums = [times(g, chosen(mslots, i)) for i, g in zip(rows, resid)]
        for i, z in zip(rows, sums):
            v["mpiece"][i] = z

    for_rows(0, mcount, mid_pieces)

    whole_zero = jnp.zeros(mrhs.shape[1:], F32)
    low_first = blk * 2 * half

    def low_terms(c):
        total = whole_zero
        for j in range(mcount):
            total = total + jnp.where(low[j] - low_first == c, v["mpiece"][j], whole_zero)
        place = c // half
        row = lax.rem(c, half)
        for g in range(groups):
            v["fold_out"][2 * g + place, row] = total[
                g * wide_r : (g + 1) * wide_r
            ].astype(BF16)

    each(0, 2 * half, low_terms)

    fold_copies = [
        remote(
            v["fold_out"].at[along_fold(k)[0]],
            v["fold_in"].at[k],
            q["fold_send"].at[k],
            q["fold_recv"].at[k],
            along_fold(k),
        )
        for k in range(1, folds)
    ]
    send(fold_copies)
    v["fold_in"][0] = v["fold_out"][fold]
    for copy in later[2:]:
        copy.wait()
    received(fold_copies)
    total = v["fold_in"][0].astype(F32)
    for k in range(1, folds):
        total = total + v["fold_in"][k].astype(F32)
    crhs[...] = total

    mine = 2 * half + core * half
    other = fold + 1 - 2 * core
    piece_rows_c = half // group_of(half, SPLIT)

    def coarse_copies(turn):
        wide = w["cwide"][turn]
        copies = []
        place = 0
        for step, offset in ((1, 0), (-1, 2), (0, 1)):
            for device in (other,) if step == 0 else (fold, other):
                for part in range(half // piece_rows_c):
                    rows = part * piece_rows_c
                    copies.append(
                        remote(
                            wide.at[pl.ds(mine + rows, piece_rows_c)],
                            wide.at[
                                pl.ds(
                                    offset * 2 * half + core * half + rows, piece_rows_c
                                )
                            ],
                            q["coarse_send"].at[turn, place],
                            q["coarse_recv"].at[turn, place],
                            (device, lax.rem(blk + step + blks, blks)),
                        )
                    )
                    place += 1
        return copies

    def coarse_put(turn, rows, fresh):
        for i, z in zip(rows, fresh):
            cfield[i] = z
            w["cwide"][turn][mine + i] = z.astype(BF16)

    def coarse_first(rows):
        coarse_put(0, rows, [times(crhs[i].astype(BF16), csmo[i]) for i in rows])

    for_rows(0, half, coarse_first)
    for turn in range(COARSE - 1):
        wide = w["cwide"][turn]
        copies = coarse_copies(turn)
        send(copies)

        def coarse_own(rows):
            fresh = [crhs[i] - low_level.own(i, wide[mine + i]) for i in rows]
            for i, z in zip(rows, fresh):
                v["cbase"][i] = z

        for_rows(0, half, coarse_own)
        received(copies)

        def coarse_sweep(rows):
            resid = [
                (v["cbase"][i] - low_level.others(i, wide)).astype(BF16) for i in rows
            ]
            fresh = [cfield[i] + times(g, csmo[i]) for i, g in zip(rows, resid)]
            coarse_put(turn + 1, rows, fresh)

        for_rows(0, half, coarse_sweep)

    last_own = w["cwide"][COARSE - 1]
    gather_copies = [
        remote(
            last_own.at[pl.ds(mine, half)],
            v["gathered"].at[fold],
            q["gather_send"].at[k],
            q["gather_recv"].at[k],
            along_fold(k),
        )
        for k in range(1, folds)
    ]
    send(gather_copies)
    v["gathered"][fold] = last_own[pl.ds(mine, half)]
    received(gather_copies)
    for f in range(folds):
        g, place = f // 2, f % 2
        v["coarse"][pl.ds(place * half, half), pl.ds(g * wide_r, wide_r), :] = v[
            "gathered"
        ][f].astype(F32)
    keeps = [pltpu.make_async_copy(v["coarse"], coarse_o, q["keep"].at[0])]
    keeps[-1].start()

    def mid_lift(rows):
        lifted = [
            jnp.dot(
                v["coarse"][within(low[i] - low_first, 2 * half)].astype(BF16),
                chosen(mslots, i),
                preferred_element_type=F32,
            )
            for i in rows
        ]
        mid_put(2, rows, [mpre[i] + z for i, z in zip(rows, lifted)])

    for_rows(0, mcount, mid_lift)
    mid_exchange(2)

    def mid_last(rows):
        resid = [mid_resid(2, i) for i in rows]
        fresh = [mpre[i] + times(g, msmo[i]) for i, g in zip(rows, resid)]
        for i, z in zip(rows, fresh):
            v["mfield"][i] = z
            for h in range(HALVES):
                w["mround"][h][i] = z[h * rh : (h + 1) * rh].astype(BF16)

    for_rows(0, mcount, mid_last)

    def back_copy(h, k):
        return remote(
            w["backout"][h].at[k],
            w["backbox"][h].at[pl.ds(k * CAP, CAP)],
            q["back_send"].at[h, k],
            q["back_recv"].at[h, k],
            along_blk(k),
        )

    for h in range(HALVES):

        def wanted(k, s):
            place = goals[lax.rem(blks - k, blks), s, 0]
            return w["mround"][h][within(place, mcount)]

        def pack_back(k):
            for s in range(CAP):
                w["backout"][h][k, s] = wanted(k, s)
            back_copy(h, k).start()

        each(1, blks, pack_back)
        for s in range(CAP):
            w["backbox"][h][s] = wanted(0, s)
    keeps.append(pltpu.make_async_copy(v["mfield"], mid_o, q["keep"].at[1]))
    keeps[-1].start()

    for h in range(HALVES):
        each(1, blks, lambda k: back_copy(h, k).wait_recv())
        for part in range(PARTS):

            def fine_lift(rows):
                lifted = [
                    jnp.dot(
                        w["backbox"][h][within(v["places_s"][0, i], blks * CAP)],
                        chosen(slots, i),
                        preferred_element_type=F32,
                    )
                    for i in rows
                ]
                fresh = [pre[i, part_of_r(h), :] + z for i, z in zip(rows, lifted)]
                for i, z in zip(rows, fresh):
                    pre[i, part_of_r(h), :] = z
                    fine_wide(2, h)[count + i] = z.astype(BF16)

            for_rows(part * chunk, chunk, fine_lift)
            send(fine_halo(2, h, part))
    for h in range(HALVES):
        fine_own(2, h)
    for h in range(HALVES):
        fine_received(2, h)
        for part in range(PARTS):

            def fine_last(rows):
                resid = [fine_resid(2, h, i) for i in rows]
                fresh = [
                    pre[i, part_of_r(h), :] + times(g, smo[i])
                    for i, g in zip(rows, resid)
                ]
                for i, z in zip(rows, fresh):
                    pre[i, part_of_r(h), :] = z

            for_rows(part * chunk, chunk, fine_last)
            if h == HALVES - 1:
                rows = pl.ds(part * chunk, chunk)
                keeps.append(
                    pltpu.make_async_copy(
                        pre.at[rows], fine_o.at[rows], q["keep"].at[2 + part]
                    )
                )
                keeps[-1].start()

    for copy in sent:
        copy.wait_send()

    def end_sends(k):
        goal_copy(k).wait_send()
        for h in range(HALVES):
            piece_copy(h, k).wait_send()
            back_copy(h, k).wait_send()

    each(1, blks, end_sends)
    for copy in keeps:
        copy.wait()


def on_device(
    fine_rhs,
    fine_tiles,
    fine_cols,
    fine_smoother,
    fine_map,
    fine_slots,
    mid_tiles,
    mid_cols,
    mid_smoother,
    mid_map,
    mid_slots,
    coarse_tiles,
    coarse_cols,
    coarse_smoother,
):
    count, stored, width, _ = fine_tiles.shape
    mcount = mid_tiles.shape[0]
    lcount = coarse_tiles.shape[0]
    r = fine_rhs.shape[1]
    folds, blks = lax.axis_size("fold"), lax.axis_size("blk")
    half = lcount // 2
    rh, wide_r = r // HALVES, r * 2 // folds

    dma = pltpu.SemaphoreType.DMA

    def field(blocks, rows=r, kind=F32):
        return pltpu.VMEM((blocks, rows, width), kind)

    def tile(blocks, *more):
        return pltpu.VMEM((blocks, *more, width, width), BF16)

    arrays = {
        "tiles": tile(count, stored),
        "smo": tile(count),
        "rhs": field(count),
        "pre": field(count),
        "mtiles": tile(mcount, stored),
        "msmo": tile(mcount),
        "mrhs": field(mcount),
        "mpre": field(mcount),
        "mbase": field(mcount),
        "mpiece": field(mcount),
        "mfield": field(mcount),
        "ctiles": tile(half, stored),
        "csmo": tile(half),
        "crhs": field(half, wide_r),
        "cfield": field(half, wide_r),
        "cbase": field(half, wide_r),
        "fold_out": pltpu.VMEM((folds, half, wide_r, width), BF16),
        "fold_in": pltpu.VMEM((folds, half, wide_r, width), BF16),
        "gathered": pltpu.VMEM((folds, half, wide_r, width), BF16),
        "coarse": field(lcount),
        "table": pltpu.VMEM((blks, SLOTS, 128), I32),
        "goals": pltpu.VMEM((blks, SLOTS, 128), I32),
        "places": pltpu.VMEM((SLOTS, 128), I32),
        "table_s": pltpu.SMEM((blks, SLOTS, 128), I32),
        "goals_s": pltpu.SMEM((blks, SLOTS, 128), I32),
        "places_s": pltpu.SMEM((SLOTS, 128), I32),
    }
    box = pltpu.VMEM((blks, CAP, rh, width), BF16)
    several = {
        "wide": [field(3 * count, rh, BF16)] * (3 * HALVES),
        "base": [field(count, rh)] * HALVES,
        "piece": [field(count, rh, BF16)] * HALVES,
        "outbox": [box] * HALVES,
        "inbox": [box] * HALVES,
        "backout": [box] * HALVES,
        "backbox": [field(blks * CAP, rh, BF16)] * HALVES,
        "mwide": [field(3 * mcount, r, BF16)] * 3,
        "mround": [field(mcount, rh, BF16)] * HALVES,
        "cwide": [field(3 * lcount, wide_r, BF16)] * COARSE,
    }
    sems = {
        "load": dma((2 * PARTS + 5,)),
        "small": dma((3,)),
        "keep": dma((2 + PARTS,)),
    }
    for name, shape in (
        ("halo", (3 * HALVES * PARTS, 2)),
        ("mid", (3, 2)),
        ("goal", (blks,)),
        ("piece", (HALVES, blks)),
        ("back", (HALVES, blks)),
        ("fold", (folds,)),
        ("gather", (folds,)),
        ("coarse", (COARSE - 1, 5 * SPLIT)),
    ):
        sems[name + "_send"] = dma(shape)
        sems[name + "_recv"] = dma(shape)

    smem = pl.BlockSpec(memory_space=pltpu.SMEM)
    vmem = pl.BlockSpec(memory_space=pltpu.VMEM)
    hbm = pl.BlockSpec(memory_space=pltpu.HBM)
    return pl.pallas_call(
        cycle,
        out_shape=(
            jax.ShapeDtypeStruct((count, r, width), F32),
            jax.ShapeDtypeStruct((mcount, r, width), F32),
            jax.ShapeDtypeStruct((lcount, r, width), F32),
        ),
        in_specs=[smem] * 4 + [vmem] * 3 + [hbm] * 7,
        out_specs=(hbm, hbm, hbm),
        scratch_shapes=[arrays, several, sems],
        compiler_params=pltpu.CompilerParams(
            collective_id=1, has_side_effects=True, vmem_limit_bytes=56 << 20
        ),
        name="cycle",
    )(
        fine_cols.T,
        mid_cols.T,
        coarse_cols.T,
        mid_map,
        fine_map.reshape(1, count),
        fine_slots,
        mid_slots,
        fine_rhs,
        fine_tiles,
        fine_smoother,
        mid_tiles,
        mid_smoother,
        coarse_tiles,
        coarse_smoother,
    )


def solution(mesh):
    both = ("fold", "blk")
    placed = (
        P(both, None, None),
        P(both, None, None, None),
        P(both, None),
        P(both, None, None),
        P(both),
        P(both, None),
        P(both, None, None, None),
        P(both, None),
        P(both, None, None),
        P(both),
        P(both, None),
        P("blk", None, None, None),
        P("blk", None),
        P("blk", None, None),
    )
    return jax.shard_map(
        on_device,
        mesh=mesh,
        in_specs=placed,
        out_specs=(P(both, None, None), P(both, None, None), P("blk", None, None)),
        check_vma=False,
    )
```

```python
import jax
import jax.numpy as jnp
from jax import lax
from jax.experimental import pallas as pl
from jax.experimental.pallas import tpu as pltpu
from jax.sharding import PartitionSpec as P

COARSE = 8
CAP = 3
HALVES = 2
PARTS = 2
SPLIT = 2
SLOTS = 8
MESH = pl.DeviceIdType.MESH
F32 = jnp.float32
BF16 = jnp.bfloat16
I32 = jnp.int32


def times(left, right):
    return lax.dot_general(
        left, right, (((1,), (1,)), ((), ())), preferred_element_type=F32
    )


def group_of(count, most):
    return max(size for size in range(1, most + 1) if count % size == 0)


def for_rows(start, count, body, most=12):
    size = group_of(count, most)

    def step(turn, carry):
        first = start + turn * size
        body([first + k for k in range(size)])
        return carry

    lax.fori_loop(0, count // size, step, 0)


def each(first, last, body):
    def step(k, carry):
        body(k)
        return carry

    lax.fori_loop(first, last, step, 0)


def chosen(slots, row):
    line = slots[pl.ds(row, 1), :]
    width = line.shape[1]
    places = lax.broadcasted_iota(I32, (width, width), 0)
    return jnp.where(places == line, 1.0, 0.0).astype(BF16)


def remote(source, target, send, recv, device):
    return pltpu.make_async_remote_copy(
        src_ref=source,
        dst_ref=target,
        send_sem=send,
        recv_sem=recv,
        device_id=device,
        device_id_type=MESH,
    )


def within(index, size):
    return jnp.minimum(jnp.maximum(index, 0), size - 1)


class Level:
    def __init__(self, tiles, cols, first, span, start=0):
        self.tiles, self.cols, self.start = tiles, cols, start
        self.first, self.span = first, span

    def own(self, row, value):
        return times(value, self.tiles[row, 0])

    def others(self, row, wide):
        stored = self.tiles.shape[1]
        picked = []
        for k in range(1, stored):
            at = self.cols[k, self.start + row] - self.first
            at = jnp.where(at < 0, at + self.span, at)
            at = jnp.where(at >= self.span, at - self.span, at)
            picked.append(wide[within(at, wide.shape[0])])
        tile = jnp.concatenate([self.tiles[row, k] for k in range(1, stored)], axis=1)
        return times(jnp.concatenate(picked, axis=1), tile)


def cycle(
    fcols,
    mcols,
    ccols,
    low,
    fmap,
    slots,
    mslots,
    rhs_h,
    tiles_h,
    smo_h,
    mtiles_h,
    msmo_h,
    ctiles_h,
    csmo_h,
    fine_o,
    mid_o,
    coarse_o,
    v,
    w,
    q,
):
    fold, blk = lax.axis_index("fold"), lax.axis_index("blk")
    folds, blks = lax.axis_size("fold"), lax.axis_size("blk")
    tiles, smo, rhs, pre = v["tiles"], v["smo"], v["rhs"], v["pre"]
    mtiles, msmo, mrhs, mpre = v["mtiles"], v["msmo"], v["mrhs"], v["mpre"]
    ctiles, csmo, crhs, cfield = v["ctiles"], v["csmo"], v["crhs"], v["cfield"]
    count, mcount, half = tiles.shape[0], mtiles.shape[0], ctiles.shape[0]
    rh = rhs.shape[1] // HALVES
    chunk = count // PARTS
    wide_r = crhs.shape[1]
    groups = folds // 2
    core = lax.rem(fold, 2)
    sent = []

    def along_blk(step):
        return (fold, lax.rem(blk + step + blks, blks))

    def along_fold(step):
        return (lax.rem(fold + step, folds), blk)

    def load(source, target, place, start=0, rows=None):
        if rows is not None:
            source, target = source.at[pl.ds(start, rows)], target.at[pl.ds(start, rows)]
        return pltpu.make_async_copy(source, target, q["load"].at[place])

    first_loads = []
    for part in range(PARTS):
        first_loads.append(load(rhs_h, rhs, 2 * part, part * chunk, chunk))
        first_loads.append(load(smo_h, smo, 2 * part + 1, part * chunk, chunk))
    tile_load = load(tiles_h, tiles, 2 * PARTS)
    later = [
        load(msmo_h, msmo, 2 * PARTS + 1),
        load(mtiles_h, mtiles, 2 * PARTS + 2),
        load(csmo_h.at[pl.ds(core * half, half)], csmo, 2 * PARTS + 3),
        load(ctiles_h.at[pl.ds(core * half, half)], ctiles, 2 * PARTS + 4),
    ]
    for copy in first_loads + [tile_load]:
        copy.start()

    barrier = pltpu.get_barrier_semaphore()

    def greet(device):
        pl.semaphore_signal(barrier, inc=1, device_id=device, device_id_type=MESH)

    for step in (1, -1):
        greet(along_blk(step))
        greet(along_fold(step + folds))

    def spread(along, size, first):
        stages, reach = [], 1
        while 2 * reach < size:
            stages.append((along, reach, size, first + len(stages)))
            reach *= 2
        return stages

    def spread_stage(stage):
        along, reach, size, place = stage
        for step in (reach, size - reach):
            pl.semaphore_signal(
                q["news"].at[place], inc=1, device_id=along(step), device_id_type=MESH
            )
        pl.semaphore_wait(q["news"].at[place], 2)

    blk_news = spread(along_blk, blks, 0)
    fold_news = spread(along_fold, folds, len(blk_news))

    fine = Level(tiles, fcols, (fold * blks + blk - 1) * count, blks * count)
    mid = Level(mtiles, mcols, (fold * blks + blk - 1) * mcount, blks * mcount)
    low_level = Level(
        ctiles, ccols, (blk - 1) * 2 * half, blks * 2 * half, core * half
    )

    def halo(wide, size, start, rows, sems, place):
        own = wide.at[pl.ds(size + start, rows)]
        return [
            remote(
                own,
                wide.at[pl.ds(at + start, rows)],
                q[sems + "_send"].at[place, side],
                q[sems + "_recv"].at[place, side],
                along_blk(step),
            )
            for side, (at, step) in enumerate(((0, 1), (2 * size, -1)))
        ]

    def send(copies):
        for copy in copies:
            copy.start()
        sent.extend(copies)

    def received(copies):
        for copy in copies:
            copy.wait_recv()

    def fine_halo(turn, h, part):
        place = (turn * HALVES + h) * PARTS + part
        return halo(w["wide"][turn * HALVES + h], count, part * chunk, chunk, "halo", place)

    def fine_wide(turn, h):
        return w["wide"][turn * HALVES + h]

    def fine_received(turn, h):
        for part in range(PARTS):
            received(fine_halo(turn, h, part))

    def part_of_r(h):
        return pl.ds(h * rh, rh)

    for part in range(PARTS):
        first_loads[2 * part].wait()
        first_loads[2 * part + 1].wait()

        def first_rows(rows):
            fresh = [times(rhs[i].astype(BF16), smo[i]) for i in rows]
            for i, z in zip(rows, fresh):
                pre[i] = z
                for h in range(HALVES):
                    fine_wide(0, h)[count + i] = z[h * rh : (h + 1) * rh].astype(BF16)

        for_rows(part * chunk, chunk, first_rows)
        if part == 0:
            pl.semaphore_wait(barrier, 4)
        send(fine_halo(0, 0, part))
    for h in range(1, HALVES):
        for part in range(PARTS):
            send(fine_halo(0, h, part))
    for copy in later:
        copy.start()

    line = fmap[...] - fold * blks * mcount
    owner = lax.shift_right_logical(line * (-(-(1 << 19) // mcount)), 19)
    target = line - owner * mcount
    steps = owner - blk
    steps = jnp.where(steps < 0, steps + blks, steps)
    across = lax.broadcasted_iota(I32, (count, count), 1)
    down = lax.broadcasted_iota(I32, (count, count), 0)
    steps_down = jnp.sum(jnp.where(across == down, steps, 0), axis=1, keepdims=True)
    ahead = (steps_down == steps) & (down < across)
    rank = jnp.sum(jnp.where(ahead, 1, 0), axis=0, keepdims=True)
    position = steps * SLOTS + rank
    hit = lax.broadcasted_iota(I32, (blks * SLOTS, count), 0) == position
    order = lax.broadcasted_iota(I32, (blks * SLOTS, count), 1)
    index = jnp.sum(jnp.where(hit, order, 0), axis=1, keepdims=True)
    goal = jnp.sum(jnp.where(hit, target - mcount, 0), axis=1, keepdims=True) + mcount
    lane = lax.broadcasted_iota(I32, (blks * SLOTS, 128), 1)
    table = jnp.where(lane == 0, goal, index)
    v["table"][...] = table.reshape(blks, SLOTS, 128)
    back_steps = jnp.where(steps == 0, 0, blks - steps)
    v["places"][pl.ds(0, 1), pl.ds(0, count)] = back_steps * CAP + rank

    def small(source, target, place):
        return pltpu.make_async_copy(source, target, q["small"].at[place])

    own_table = small(v["table"], v["table_s"], 0)
    own_places = small(v["places"], v["places_s"], 1)
    own_table.start()
    own_places.start()

    def goal_copy(k):
        return remote(
            v["table"].at[k],
            v["goals"].at[k],
            q["goal_send"].at[k],
            q["goal_recv"].at[k],
            along_blk(k),
        )

    v["goals"][0] = v["table"][0]

    def fine_own(turn, h):
        def rows_of(rows):
            fresh = [
                rhs[i, part_of_r(h), :] - fine.own(i, fine_wide(turn, h)[count + i])
                for i in rows
            ]
            for i, z in zip(rows, fresh):
                w["base"][h][i] = z

        for_rows(0, count, rows_of)

    def fine_resid(turn, h, i):
        return (w["base"][h][i] - fine.others(i, fine_wide(turn, h))).astype(BF16)

    tile_load.wait()
    for stage in blk_news[:2]:
        spread_stage(stage)
    for h in range(HALVES):
        fine_own(0, h)
    for stage in blk_news[2:]:
        spread_stage(stage)
    each(1, blks, lambda k: goal_copy(k).start())

    for h in range(HALVES):
        fine_received(0, h)
        for part in range(PARTS):

            def sweep_rows(rows):
                resid = [fine_resid(0, h, i) for i in rows]
                fresh = [
                    pre[i, part_of_r(h), :] + times(g, smo[i])
                    for i, g in zip(rows, resid)
                ]
                for i, z in zip(rows, fresh):
                    pre[i, part_of_r(h), :] = z
                    fine_wide(1, h)[count + i] = z.astype(BF16)

            for_rows(part * chunk, chunk, sweep_rows)
            send(fine_halo(1, h, part))
    for h in range(HALVES):
        fine_own(1, h)
    for stage in fold_news:
        spread_stage(stage)
    own_table.wait()
    own_places.wait()

    def piece_copy(h, k):
        return remote(
            w["outbox"][h].at[k],
            w["inbox"][h].at[k],
            q["piece_send"].at[h, k],
            q["piece_recv"].at[h, k],
            along_blk(k),
        )

    for h in range(HALVES):
        fine_received(1, h)
        piece = w["piece"][h]

        def piece_rows(rows):
            resid = [fine_resid(1, h, i) for i in rows]
            sums = [times(g, chosen(slots, i)) for i, g in zip(rows, resid)]
            for i, z in zip(rows, sums):
                piece[i] = z.astype(BF16)

        for_rows(0, count, piece_rows)

        def pack(k):
            for s in range(CAP):
                w["outbox"][h][k, s] = piece[within(v["table_s"][k, s, 1], count)]
            piece_copy(h, k).start()

        each(1, blks, pack)
        for s in range(CAP):
            w["inbox"][h][0, s] = piece[within(v["table_s"][0, s, 1], count)]

    each(1, blks, lambda k: goal_copy(k).wait_recv())
    goals_move = small(v["goals"], v["goals_s"], 2)
    goals_move.start()
    goals_move.wait()
    goals = v["goals_s"]

    zero = jnp.zeros((rh, rhs.shape[2]), F32)
    tied = group_of(mcount, 12)
    for h in range(HALVES):
        for first in range(0, mcount, tied):

            def add_pieces(k, sums, wait=True):
                if wait and first == 0:
                    piece_copy(h, k).wait_recv()
                for s in range(CAP):
                    value = w["inbox"][h][k, s].astype(F32)
                    place = goals[k, s, 0]
                    sums = tuple(
                        total + jnp.where(place == first + t, value, zero)
                        for t, total in enumerate(sums)
                    )
                return sums

            sums = add_pieces(0, (zero,) * tied, wait=False)
            sums = lax.fori_loop(1, blks, add_pieces, sums)
            for t, total in enumerate(sums):
                mrhs[first + t, part_of_r(h), :] = total
    for copy in later[:2]:
        copy.wait()

    def mid_put(turn, rows, fresh):
        for i, z in zip(rows, fresh):
            mpre[i] = z
            w["mwide"][turn][mcount + i] = z.astype(BF16)

    def mid_first(rows):
        mid_put(0, rows, [times(mrhs[i].astype(BF16), msmo[i]) for i in rows])

    def mid_exchange(turn):
        wide = w["mwide"][turn]
        copies = halo(wide, mcount, 0, mcount, "mid", turn)
        send(copies)

        def own_rows(rows):
            fresh = [mrhs[i] - mid.own(i, wide[mcount + i]) for i in rows]
            for i, z in zip(rows, fresh):
                v["mbase"][i] = z

        for_rows(0, mcount, own_rows)
        received(copies)

    def mid_resid(turn, i):
        return (v["mbase"][i] - mid.others(i, w["mwide"][turn])).astype(BF16)

    for_rows(0, mcount, mid_first)
    mid_exchange(0)

    def mid_sweep(rows):
        resid = [mid_resid(0, i) for i in rows]
        mid_put(1, rows, [mpre[i] + times(g, msmo[i]) for i, g in zip(rows, resid)])

    for_rows(0, mcount, mid_sweep)
    mid_exchange(1)

    def mid_pieces(rows):
        resid = [mid_resid(1, i) for i in rows]
        sums = [times(g, chosen(mslots, i)) for i, g in zip(rows, resid)]
        for i, z in zip(rows, sums):
            v["mpiece"][i] = z

    for_rows(0, mcount, mid_pieces)

    whole_zero = jnp.zeros(mrhs.shape[1:], F32)
    low_first = blk * 2 * half

    def low_terms(c):
        total = whole_zero
        for j in range(mcount):
            total = total + jnp.where(low[j] - low_first == c, v["mpiece"][j], whole_zero)
        place = c // half
        row = lax.rem(c, half)
        for g in range(groups):
            v["fold_out"][2 * g + place, row] = total[
                g * wide_r : (g + 1) * wide_r
            ].astype(BF16)

    each(0, 2 * half, low_terms)

    fold_copies = [
        remote(
            v["fold_out"].at[along_fold(k)[0]],
            v["fold_in"].at[k],
            q["fold_send"].at[k],
            q["fold_recv"].at[k],
            along_fold(k),
        )
        for k in range(1, folds)
    ]
    send(fold_copies)
    v["fold_in"][0] = v["fold_out"][fold]
    for copy in later[2:]:
        copy.wait()
    received(fold_copies)
    total = v["fold_in"][0].astype(F32)
    for k in range(1, folds):
        total = total + v["fold_in"][k].astype(F32)
    crhs[...] = total

    mine = 2 * half + core * half
    other = fold + 1 - 2 * core
    piece_rows_c = half // group_of(half, SPLIT)

    def coarse_copies(turn):
        wide = w["cwide"][turn]
        copies = []
        place = 0
        for step, offset in ((1, 0), (-1, 2), (0, 1)):
            for device in (other,) if step == 0 else (fold, other):
                for part in range(half // piece_rows_c):
                    rows = part * piece_rows_c
                    copies.append(
                        remote(
                            wide.at[pl.ds(mine + rows, piece_rows_c)],
                            wide.at[
                                pl.ds(
                                    offset * 2 * half + core * half + rows, piece_rows_c
                                )
                            ],
                            q["coarse_send"].at[turn, place],
                            q["coarse_recv"].at[turn, place],
                            (device, lax.rem(blk + step + blks, blks)),
                        )
                    )
                    place += 1
        return copies

    def coarse_put(turn, rows, fresh):
        for i, z in zip(rows, fresh):
            cfield[i] = z
            w["cwide"][turn][mine + i] = z.astype(BF16)

    def coarse_first(rows):
        coarse_put(0, rows, [times(crhs[i].astype(BF16), csmo[i]) for i in rows])

    for_rows(0, half, coarse_first)
    for turn in range(COARSE - 1):
        wide = w["cwide"][turn]
        copies = coarse_copies(turn)
        send(copies)

        def coarse_own(rows):
            fresh = [crhs[i] - low_level.own(i, wide[mine + i]) for i in rows]
            for i, z in zip(rows, fresh):
                v["cbase"][i] = z

        for_rows(0, half, coarse_own)
        received(copies)

        def coarse_sweep(rows):
            resid = [
                (v["cbase"][i] - low_level.others(i, wide)).astype(BF16) for i in rows
            ]
            fresh = [cfield[i] + times(g, csmo[i]) for i, g in zip(rows, resid)]
            coarse_put(turn + 1, rows, fresh)

        for_rows(0, half, coarse_sweep)

    last_own = w["cwide"][COARSE - 1]
    gather_copies = [
        remote(
            last_own.at[pl.ds(mine, half)],
            v["gathered"].at[fold],
            q["gather_send"].at[k],
            q["gather_recv"].at[k],
            along_fold(k),
        )
        for k in range(1, folds)
    ]
    send(gather_copies)
    v["gathered"][fold] = last_own[pl.ds(mine, half)]
    received(gather_copies)
    for f in range(folds):
        g, place = f // 2, f % 2
        v["coarse"][pl.ds(place * half, half), pl.ds(g * wide_r, wide_r), :] = v[
            "gathered"
        ][f].astype(F32)
    keeps = [pltpu.make_async_copy(v["coarse"], coarse_o, q["keep"].at[0])]
    keeps[-1].start()

    def mid_lift(rows):
        lifted = [
            jnp.dot(
                v["coarse"][within(low[i] - low_first, 2 * half)].astype(BF16),
                chosen(mslots, i),
                preferred_element_type=F32,
            )
            for i in rows
        ]
        mid_put(2, rows, [mpre[i] + z for i, z in zip(rows, lifted)])

    for_rows(0, mcount, mid_lift)
    mid_exchange(2)

    def mid_last(rows):
        resid = [mid_resid(2, i) for i in rows]
        fresh = [mpre[i] + times(g, msmo[i]) for i, g in zip(rows, resid)]
        for i, z in zip(rows, fresh):
            v["mfield"][i] = z
            for h in range(HALVES):
                w["mround"][h][i] = z[h * rh : (h + 1) * rh].astype(BF16)

    for_rows(0, mcount, mid_last)

    def back_copy(h, k):
        return remote(
            w["backout"][h].at[k],
            w["backbox"][h].at[pl.ds(k * CAP, CAP)],
            q["back_send"].at[h, k],
            q["back_recv"].at[h, k],
            along_blk(k),
        )

    for h in range(HALVES):

        def wanted(k, s):
            place = goals[lax.rem(blks - k, blks), s, 0]
            return w["mround"][h][within(place, mcount)]

        def pack_back(k):
            for s in range(CAP):
                w["backout"][h][k, s] = wanted(k, s)
            back_copy(h, k).start()

        each(1, blks, pack_back)
        for s in range(CAP):
            w["backbox"][h][s] = wanted(0, s)
    keeps.append(pltpu.make_async_copy(v["mfield"], mid_o, q["keep"].at[1]))
    keeps[-1].start()

    for h in range(HALVES):
        each(1, blks, lambda k: back_copy(h, k).wait_recv())
        for part in range(PARTS):

            def fine_lift(rows):
                lifted = [
                    jnp.dot(
                        w["backbox"][h][within(v["places_s"][0, i], blks * CAP)],
                        chosen(slots, i),
                        preferred_element_type=F32,
                    )
                    for i in rows
                ]
                fresh = [pre[i, part_of_r(h), :] + z for i, z in zip(rows, lifted)]
                for i, z in zip(rows, fresh):
                    pre[i, part_of_r(h), :] = z
                    fine_wide(2, h)[count + i] = z.astype(BF16)

            for_rows(part * chunk, chunk, fine_lift)
            send(fine_halo(2, h, part))
    for h in range(HALVES):
        fine_own(2, h)
    for h in range(HALVES):
        fine_received(2, h)
        for part in range(PARTS):

            def fine_last(rows):
                resid = [fine_resid(2, h, i) for i in rows]
                fresh = [
                    pre[i, part_of_r(h), :] + times(g, smo[i])
                    for i, g in zip(rows, resid)
                ]
                for i, z in zip(rows, fresh):
                    pre[i, part_of_r(h), :] = z

            for_rows(part * chunk, chunk, fine_last)
            if h == HALVES - 1:
                rows = pl.ds(part * chunk, chunk)
                keeps.append(
                    pltpu.make_async_copy(
                        pre.at[rows], fine_o.at[rows], q["keep"].at[2 + part]
                    )
                )
                keeps[-1].start()

    for copy in sent:
        copy.wait_send()

    def end_sends(k):
        goal_copy(k).wait_send()
        for h in range(HALVES):
            piece_copy(h, k).wait_send()
            back_copy(h, k).wait_send()

    each(1, blks, end_sends)
    for copy in keeps:
        copy.wait()


def on_device(
    fine_rhs,
    fine_tiles,
    fine_cols,
    fine_smoother,
    fine_map,
    fine_slots,
    mid_tiles,
    mid_cols,
    mid_smoother,
    mid_map,
    mid_slots,
    coarse_tiles,
    coarse_cols,
    coarse_smoother,
):
    count, stored, width, _ = fine_tiles.shape
    mcount = mid_tiles.shape[0]
    lcount = coarse_tiles.shape[0]
    r = fine_rhs.shape[1]
    folds, blks = lax.axis_size("fold"), lax.axis_size("blk")
    half = lcount // 2
    rh, wide_r = r // HALVES, r * 2 // folds

    dma = pltpu.SemaphoreType.DMA

    def field(blocks, rows=r, kind=F32):
        return pltpu.VMEM((blocks, rows, width), kind)

    def tile(blocks, *more):
        return pltpu.VMEM((blocks, *more, width, width), BF16)

    arrays = {
        "tiles": tile(count, stored),
        "smo": tile(count),
        "rhs": field(count),
        "pre": field(count),
        "mtiles": tile(mcount, stored),
        "msmo": tile(mcount),
        "mrhs": field(mcount),
        "mpre": field(mcount),
        "mbase": field(mcount),
        "mpiece": field(mcount),
        "mfield": field(mcount),
        "ctiles": tile(half, stored),
        "csmo": tile(half),
        "crhs": field(half, wide_r),
        "cfield": field(half, wide_r),
        "cbase": field(half, wide_r),
        "fold_out": pltpu.VMEM((folds, half, wide_r, width), BF16),
        "fold_in": pltpu.VMEM((folds, half, wide_r, width), BF16),
        "gathered": pltpu.VMEM((folds, half, wide_r, width), BF16),
        "coarse": field(lcount),
        "table": pltpu.VMEM((blks, SLOTS, 128), I32),
        "goals": pltpu.VMEM((blks, SLOTS, 128), I32),
        "places": pltpu.VMEM((SLOTS, 128), I32),
        "table_s": pltpu.SMEM((blks, SLOTS, 128), I32),
        "goals_s": pltpu.SMEM((blks, SLOTS, 128), I32),
        "places_s": pltpu.SMEM((SLOTS, 128), I32),
    }
    box = pltpu.VMEM((blks, CAP, rh, width), BF16)
    several = {
        "wide": [field(3 * count, rh, BF16)] * (3 * HALVES),
        "base": [field(count, rh)] * HALVES,
        "piece": [field(count, rh, BF16)] * HALVES,
        "outbox": [box] * HALVES,
        "inbox": [box] * HALVES,
        "backout": [box] * HALVES,
        "backbox": [field(blks * CAP, rh, BF16)] * HALVES,
        "mwide": [field(3 * mcount, r, BF16)] * 3,
        "mround": [field(mcount, rh, BF16)] * HALVES,
        "cwide": [field(3 * lcount, wide_r, BF16)] * COARSE,
    }
    sems = {
        "load": dma((2 * PARTS + 5,)),
        "small": dma((3,)),
        "keep": dma((2 + PARTS,)),
        "news": pltpu.SemaphoreType.REGULAR((8,)),
    }
    for name, shape in (
        ("halo", (3 * HALVES * PARTS, 2)),
        ("mid", (3, 2)),
        ("goal", (blks,)),
        ("piece", (HALVES, blks)),
        ("back", (HALVES, blks)),
        ("fold", (folds,)),
        ("gather", (folds,)),
        ("coarse", (COARSE - 1, 5 * SPLIT)),
    ):
        sems[name + "_send"] = dma(shape)
        sems[name + "_recv"] = dma(shape)

    smem = pl.BlockSpec(memory_space=pltpu.SMEM)
    vmem = pl.BlockSpec(memory_space=pltpu.VMEM)
    hbm = pl.BlockSpec(memory_space=pltpu.HBM)
    anywhere = pl.BlockSpec(memory_space=pl.ANY)
    return pl.pallas_call(
        cycle,
        out_shape=(
            jax.ShapeDtypeStruct((count, r, width), F32),
            jax.ShapeDtypeStruct((mcount, r, width), F32),
            jax.ShapeDtypeStruct((lcount, r, width), F32),
        ),
        in_specs=[smem] * 4 + [vmem] * 3 + [hbm] * 7,
        out_specs=(anywhere, anywhere, anywhere),
        scratch_shapes=[arrays, several, sems],
        compiler_params=pltpu.CompilerParams(
            collective_id=1, has_side_effects=True, vmem_limit_bytes=44 << 20
        ),
        name="cycle",
    )(
        fine_cols.T,
        mid_cols.T,
        coarse_cols.T,
        mid_map,
        fine_map.reshape(1, count),
        fine_slots,
        mid_slots,
        fine_rhs,
        fine_tiles,
        fine_smoother,
        mid_tiles,
        mid_smoother,
        coarse_tiles,
        coarse_smoother,
    )


def solution(mesh):
    both = ("fold", "blk")
    placed = (
        P(both, None, None),
        P(both, None, None, None),
        P(both, None),
        P(both, None, None),
        P(both),
        P(both, None),
        P(both, None, None, None),
        P(both, None),
        P(both, None, None),
        P(both),
        P(both, None),
        P("blk", None, None, None),
        P("blk", None),
        P("blk", None, None),
    )
    return jax.shard_map(
        on_device,
        mesh=mesh,
        in_specs=placed,
        out_specs=(P(both, None, None), P(both, None, None), P("blk", None, None)),
        check_vma=False,
    )
```

```python
import jax
import jax.numpy as jnp
from jax import lax
from jax.experimental import pallas as pl
from jax.experimental.pallas import tpu as pltpu
from jax.sharding import PartitionSpec as P

COARSE = 8
CAP = 3
HALVES = 2
PARTS = 2
SPLIT = 2
SLOTS = 8
MESH = pl.DeviceIdType.MESH
F32 = jnp.float32
BF16 = jnp.bfloat16
I32 = jnp.int32


def times(left, right):
    return lax.dot_general(
        left, right, (((1,), (1,)), ((), ())), preferred_element_type=F32
    )


def group_of(count, most):
    return max(size for size in range(1, most + 1) if count % size == 0)


def for_rows(start, count, body, most=12):
    size = group_of(count, most)

    def step(turn, carry):
        first = start + turn * size
        body([first + k for k in range(size)])
        return carry

    lax.fori_loop(0, count // size, step, 0)


def each(first, last, body):
    def step(k, carry):
        body(k)
        return carry

    lax.fori_loop(first, last, step, 0)


def chosen(slots, row):
    line = slots[pl.ds(row, 1), :]
    width = line.shape[1]
    places = lax.broadcasted_iota(I32, (width, width), 0)
    return jnp.where(places == line, 1.0, 0.0).astype(BF16)


def remote(source, target, send, recv, device):
    return pltpu.make_async_remote_copy(
        src_ref=source,
        dst_ref=target,
        send_sem=send,
        recv_sem=recv,
        device_id=device,
        device_id_type=MESH,
    )


def within(index, size):
    return jnp.minimum(jnp.maximum(index, 0), size - 1)


class Level:
    def __init__(self, tiles, cols, first, span, start=0):
        self.tiles, self.cols, self.start = tiles, cols, start
        self.first, self.span = first, span

    def own(self, row, value):
        return times(value, self.tiles[row, 0])

    def others(self, row, wide):
        stored = self.tiles.shape[1]
        picked = []
        for k in range(1, stored):
            at = self.cols[k, self.start + row] - self.first
            at = jnp.where(at < 0, at + self.span, at)
            at = jnp.where(at >= self.span, at - self.span, at)
            picked.append(wide[within(at, wide.shape[0])])
        tile = jnp.concatenate([self.tiles[row, k] for k in range(1, stored)], axis=1)
        return times(jnp.concatenate(picked, axis=1), tile)


def cycle(
    fcols_h,
    mcols_h,
    ccols_h,
    low_h,
    fmap_h,
    slots_h,
    mslots_h,
    rhs_h,
    tiles_h,
    smo_h,
    mtiles_h,
    msmo_h,
    ctiles_h,
    csmo_h,
    fine_o,
    mid_o,
    coarse_o,
    v,
    w,
    q,
):
    fold, blk = lax.axis_index("fold"), lax.axis_index("blk")
    folds, blks = lax.axis_size("fold"), lax.axis_size("blk")
    tiles, smo, rhs, pre = v["tiles"], v["smo"], v["rhs"], v["pre"]
    mtiles, msmo, mrhs, mpre = v["mtiles"], v["msmo"], v["mrhs"], v["mpre"]
    ctiles, csmo, crhs, cfield = v["ctiles"], v["csmo"], v["crhs"], v["cfield"]
    count, mcount, half = tiles.shape[0], mtiles.shape[0], ctiles.shape[0]
    rh = rhs.shape[1] // HALVES
    chunk = count // PARTS
    wide_r = crhs.shape[1]
    groups = folds // 2
    core = lax.rem(fold, 2)
    sent = []

    def along_blk(step):
        return (fold, lax.rem(blk + step + blks, blks))

    def along_fold(step):
        return (lax.rem(fold + step, folds), blk)

    def load(source, target, place, start=0, rows=None):
        if rows is not None:
            source, target = source.at[pl.ds(start, rows)], target.at[pl.ds(start, rows)]
        return pltpu.make_async_copy(source, target, q["load"].at[place])

    first_loads = []
    for part in range(PARTS):
        first_loads.append(load(rhs_h, rhs, 2 * part, part * chunk, chunk))
        first_loads.append(load(smo_h, smo, 2 * part + 1, part * chunk, chunk))
    tile_load = load(tiles_h, tiles, 2 * PARTS)
    later = [
        load(msmo_h, msmo, 2 * PARTS + 1),
        load(mtiles_h, mtiles, 2 * PARTS + 2),
        load(csmo_h.at[pl.ds(core * half, half)], csmo, 2 * PARTS + 3),
        load(ctiles_h.at[pl.ds(core * half, half)], ctiles, 2 * PARTS + 4),
    ]
    fcols, mcols, ccols, low = v["fcols"], v["mcols"], v["ccols"], v["low"]
    fmap, slots, mslots = v["fmap"], v["slots"], v["mslots"]
    table_loads = [
        load(source, target, 2 * PARTS + 5 + k)
        for k, (source, target) in enumerate(
            (
                (fmap_h, fmap),
                (fcols_h, fcols),
                (slots_h, slots),
                (mcols_h, mcols),
                (mslots_h, mslots),
                (low_h, low),
                (ccols_h, ccols),
            )
        )
    ]
    for copy in first_loads + table_loads[:3] + [tile_load]:
        copy.start()

    barrier = pltpu.get_barrier_semaphore()

    def greet(device):
        pl.semaphore_signal(barrier, inc=1, device_id=device, device_id_type=MESH)

    for step in (1, -1):
        greet(along_blk(step))
        greet(along_fold(step + folds))

    def spread(along, size, first):
        stages, reach = [], 1
        while 2 * reach < size:
            stages.append((along, reach, size, first + len(stages)))
            reach *= 2
        return stages

    blk_news = spread(along_blk, blks, 0)
    fold_news = spread(along_fold, folds, len(blk_news))
    turns = []
    for k in range(max(len(blk_news), len(fold_news)) + 1):
        turns.append([news[k : k + 1] for news in (blk_news, fold_news)])
    pending = []

    def next_stage():
        for place in pending:
            pl.semaphore_wait(q["news"].at[place], 2)
        pending.clear()
        if turns:
            for along, reach, size, place in sum(turns.pop(0), []):
                for step in (reach, size - reach):
                    pl.semaphore_signal(
                        q["news"].at[place],
                        inc=1,
                        device_id=along(step),
                        device_id_type=MESH,
                    )
                pending.append(place)

    fine = Level(tiles, fcols, (fold * blks + blk - 1) * count, blks * count)
    mid = Level(mtiles, mcols, (fold * blks + blk - 1) * mcount, blks * mcount)
    low_level = Level(
        ctiles, ccols, (blk - 1) * 2 * half, blks * 2 * half, core * half
    )

    def halo(wide, size, start, rows, sems, place):
        own = wide.at[pl.ds(size + start, rows)]
        return [
            remote(
                own,
                wide.at[pl.ds(at + start, rows)],
                q[sems + "_send"].at[place, side],
                q[sems + "_recv"].at[place, side],
                along_blk(step),
            )
            for side, (at, step) in enumerate(((0, 1), (2 * size, -1)))
        ]

    def send(copies):
        for copy in copies:
            copy.start()
        sent.extend(copies)

    def received(copies):
        for copy in copies:
            copy.wait_recv()

    def fine_halo(turn, h, part):
        place = (turn * HALVES + h) * PARTS + part
        return halo(w["wide"][turn * HALVES + h], count, part * chunk, chunk, "halo", place)

    def fine_wide(turn, h):
        return w["wide"][turn * HALVES + h]

    def fine_received(turn, h):
        for part in range(PARTS):
            received(fine_halo(turn, h, part))

    def part_of_r(h):
        return pl.ds(h * rh, rh)

    for part in range(PARTS):
        first_loads[2 * part].wait()
        first_loads[2 * part + 1].wait()

        def first_rows(rows):
            fresh = [times(rhs[i].astype(BF16), smo[i]) for i in rows]
            for i, z in zip(rows, fresh):
                pre[i] = z
                for h in range(HALVES):
                    fine_wide(0, h)[count + i] = z[h * rh : (h + 1) * rh].astype(BF16)

        for_rows(part * chunk, chunk, first_rows)
        if part == 0:
            pl.semaphore_wait(barrier, 4)
        send(fine_halo(0, 0, part))
    for h in range(1, HALVES):
        for part in range(PARTS):
            send(fine_halo(0, h, part))
    next_stage()
    for copy in later + table_loads[3:]:
        copy.start()
    for copy in table_loads[:3]:
        copy.wait()

    line = fmap[...] - fold * blks * mcount
    owner = lax.shift_right_logical(line * (-(-(1 << 19) // mcount)), 19)
    target = line - owner * mcount
    steps = owner - blk
    steps = jnp.where(steps < 0, steps + blks, steps)
    across = lax.broadcasted_iota(I32, (count, count), 1)
    down = lax.broadcasted_iota(I32, (count, count), 0)
    steps_down = jnp.sum(jnp.where(across == down, steps, 0), axis=1, keepdims=True)
    ahead = (steps_down == steps) & (down < across)
    rank = jnp.sum(jnp.where(ahead, 1, 0), axis=0, keepdims=True)
    position = steps * SLOTS + rank
    hit = lax.broadcasted_iota(I32, (blks * SLOTS, count), 0) == position
    order = lax.broadcasted_iota(I32, (blks * SLOTS, count), 1)
    index = jnp.sum(jnp.where(hit, order, 0), axis=1, keepdims=True)
    goal = jnp.sum(jnp.where(hit, target - mcount, 0), axis=1, keepdims=True) + mcount
    lane = lax.broadcasted_iota(I32, (blks * SLOTS, 128), 1)
    table = jnp.where(lane == 0, goal, index)
    v["table"][...] = table.reshape(blks, SLOTS, 128)
    back_steps = jnp.where(steps == 0, 0, blks - steps)
    v["places"][pl.ds(0, 1), pl.ds(0, count)] = back_steps * CAP + rank

    def small(source, target, place):
        return pltpu.make_async_copy(source, target, q["small"].at[place])

    own_table = small(v["table"], v["table_s"], 0)
    own_places = small(v["places"], v["places_s"], 1)
    own_table.start()
    own_places.start()

    def goal_copy(k):
        return remote(
            v["table"].at[k],
            v["goals"].at[k],
            q["goal_send"].at[k],
            q["goal_recv"].at[k],
            along_blk(k),
        )

    v["goals"][0] = v["table"][0]

    def fine_own(turn, h):
        def rows_of(rows):
            fresh = [
                rhs[i, part_of_r(h), :] - fine.own(i, fine_wide(turn, h)[count + i])
                for i in rows
            ]
            for i, z in zip(rows, fresh):
                w["base"][h][i] = z

        for_rows(0, count, rows_of)

    def fine_resid(turn, h, i):
        return (w["base"][h][i] - fine.others(i, fine_wide(turn, h))).astype(BF16)

    tile_load.wait()
    next_stage()
    for h in range(HALVES):
        fine_own(0, h)
        next_stage()

    for h in range(HALVES):
        fine_received(0, h)
        for part in range(PARTS):

            def sweep_rows(rows):
                resid = [fine_resid(0, h, i) for i in rows]
                fresh = [
                    pre[i, part_of_r(h), :] + times(g, smo[i])
                    for i, g in zip(rows, resid)
                ]
                for i, z in zip(rows, fresh):
                    pre[i, part_of_r(h), :] = z
                    fine_wide(1, h)[count + i] = z.astype(BF16)

            for_rows(part * chunk, chunk, sweep_rows)
            send(fine_halo(1, h, part))
        next_stage()
    while turns or pending:
        next_stage()
    each(1, blks, lambda k: goal_copy(k).start())
    for h in range(HALVES):
        fine_own(1, h)
    own_table.wait()
    own_places.wait()

    def piece_copy(h, k):
        return remote(
            w["outbox"][h].at[k],
            w["inbox"][h].at[k],
            q["piece_send"].at[h, k],
            q["piece_recv"].at[h, k],
            along_blk(k),
        )

    for h in range(HALVES):
        fine_received(1, h)
        piece = w["piece"][h]

        def piece_rows(rows):
            resid = [fine_resid(1, h, i) for i in rows]
            sums = [times(g, chosen(slots, i)) for i, g in zip(rows, resid)]
            for i, z in zip(rows, sums):
                piece[i] = z.astype(BF16)

        for_rows(0, count, piece_rows)

        def pack(k):
            for s in range(CAP):
                w["outbox"][h][k, s] = piece[within(v["table_s"][k, s, 1], count)]
            piece_copy(h, k).start()

        each(1, blks, pack)
        for s in range(CAP):
            w["inbox"][h][0, s] = piece[within(v["table_s"][0, s, 1], count)]

    each(1, blks, lambda k: goal_copy(k).wait_recv())
    goals_move = small(v["goals"], v["goals_s"], 2)
    goals_move.start()
    goals_move.wait()
    goals = v["goals_s"]

    zero = jnp.zeros((rh, rhs.shape[2]), F32)
    tied = group_of(mcount, 12)
    for h in range(HALVES):
        each(1, blks, lambda k: piece_copy(h, k).wait_recv())
        for first in range(0, mcount, tied):

            def add_pieces(k, sums):
                for s in range(CAP):
                    value = w["inbox"][h][k, s].astype(F32)
                    place = goals[k, s, 0]
                    sums = tuple(
                        total + jnp.where(place == first + t, value, zero)
                        for t, total in enumerate(sums)
                    )
                return sums

            sums = lax.fori_loop(0, blks, add_pieces, (zero,) * tied)
            for t, total in enumerate(sums):
                mrhs[first + t, part_of_r(h), :] = total
    for copy in later[:2] + table_loads[3:]:
        copy.wait()

    def mid_put(turn, rows, fresh):
        for i, z in zip(rows, fresh):
            mpre[i] = z
            w["mwide"][turn][mcount + i] = z.astype(BF16)

    def mid_first(rows):
        mid_put(0, rows, [times(mrhs[i].astype(BF16), msmo[i]) for i in rows])

    def mid_exchange(turn):
        wide = w["mwide"][turn]
        copies = halo(wide, mcount, 0, mcount, "mid", turn)
        send(copies)

        def own_rows(rows):
            fresh = [mrhs[i] - mid.own(i, wide[mcount + i]) for i in rows]
            for i, z in zip(rows, fresh):
                v["mbase"][i] = z

        for_rows(0, mcount, own_rows)
        received(copies)

    def mid_resid(turn, i):
        return (v["mbase"][i] - mid.others(i, w["mwide"][turn])).astype(BF16)

    for_rows(0, mcount, mid_first)
    mid_exchange(0)

    def mid_sweep(rows):
        resid = [mid_resid(0, i) for i in rows]
        mid_put(1, rows, [mpre[i] + times(g, msmo[i]) for i, g in zip(rows, resid)])

    for_rows(0, mcount, mid_sweep)
    mid_exchange(1)

    def mid_pieces(rows):
        resid = [mid_resid(1, i) for i in rows]
        sums = [times(g, chosen(mslots, i)) for i, g in zip(rows, resid)]
        for i, z in zip(rows, sums):
            v["mpiece"][i] = z

    for_rows(0, mcount, mid_pieces)

    whole_zero = jnp.zeros(mrhs.shape[1:], F32)
    low_first = blk * 2 * half

    def low_terms(c):
        total = whole_zero
        for j in range(mcount):
            total = total + jnp.where(low[j] - low_first == c, v["mpiece"][j], whole_zero)
        place = c // half
        row = lax.rem(c, half)
        for g in range(groups):
            v["fold_out"][2 * g + place, row] = total[
                g * wide_r : (g + 1) * wide_r
            ].astype(BF16)

    each(0, 2 * half, low_terms)

    fold_copies = [
        remote(
            v["fold_out"].at[along_fold(k)[0]],
            v["fold_in"].at[k],
            q["fold_send"].at[k],
            q["fold_recv"].at[k],
            along_fold(k),
        )
        for k in range(1, folds)
    ]
    send(fold_copies)
    v["fold_in"][0] = v["fold_out"][fold]
    for copy in later[2:]:
        copy.wait()
    received(fold_copies)
    total = v["fold_in"][0].astype(F32)
    for k in range(1, folds):
        total = total + v["fold_in"][k].astype(F32)
    crhs[...] = total

    mine = 2 * half + core * half
    other = fold + 1 - 2 * core
    piece_rows_c = half // group_of(half, SPLIT)

    def coarse_copies(turn):
        wide = w["cwide"][turn]
        copies = []
        place = 0
        for step, offset in ((1, 0), (-1, 2), (0, 1)):
            for device in (other,) if step == 0 else (fold, other):
                for part in range(half // piece_rows_c):
                    rows = part * piece_rows_c
                    copies.append(
                        remote(
                            wide.at[pl.ds(mine + rows, piece_rows_c)],
                            wide.at[
                                pl.ds(
                                    offset * 2 * half + core * half + rows, piece_rows_c
                                )
                            ],
                            q["coarse_send"].at[turn, place],
                            q["coarse_recv"].at[turn, place],
                            (device, lax.rem(blk + step + blks, blks)),
                        )
                    )
                    place += 1
        return copies

    def coarse_put(turn, rows, fresh):
        for i, z in zip(rows, fresh):
            cfield[i] = z
            w["cwide"][turn][mine + i] = z.astype(BF16)

    def coarse_first(rows):
        coarse_put(0, rows, [times(crhs[i].astype(BF16), csmo[i]) for i in rows])

    for_rows(0, half, coarse_first)
    for turn in range(COARSE - 1):
        wide = w["cwide"][turn]
        copies = coarse_copies(turn)
        send(copies)

        def coarse_own(rows):
            fresh = [crhs[i] - low_level.own(i, wide[mine + i]) for i in rows]
            for i, z in zip(rows, fresh):
                v["cbase"][i] = z

        for_rows(0, half, coarse_own)
        received(copies)

        def coarse_sweep(rows):
            resid = [
                (v["cbase"][i] - low_level.others(i, wide)).astype(BF16) for i in rows
            ]
            fresh = [cfield[i] + times(g, csmo[i]) for i, g in zip(rows, resid)]
            coarse_put(turn + 1, rows, fresh)

        for_rows(0, half, coarse_sweep)

    last_own = w["cwide"][COARSE - 1]
    gather_copies = [
        remote(
            last_own.at[pl.ds(mine, half)],
            v["gathered"].at[fold],
            q["gather_send"].at[k],
            q["gather_recv"].at[k],
            along_fold(k),
        )
        for k in range(1, folds)
    ]
    send(gather_copies)
    v["gathered"][fold] = last_own[pl.ds(mine, half)]
    received(gather_copies)
    for f in range(folds):
        g, place = f // 2, f % 2
        v["coarse"][pl.ds(place * half, half), pl.ds(g * wide_r, wide_r), :] = v[
            "gathered"
        ][f].astype(F32)
    keeps = [pltpu.make_async_copy(v["coarse"], coarse_o, q["keep"].at[0])]
    keeps[-1].start()

    def mid_lift(rows):
        lifted = [
            jnp.dot(
                v["coarse"][within(low[i] - low_first, 2 * half)].astype(BF16),
                chosen(mslots, i),
                preferred_element_type=F32,
            )
            for i in rows
        ]
        mid_put(2, rows, [mpre[i] + z for i, z in zip(rows, lifted)])

    for_rows(0, mcount, mid_lift)
    mid_exchange(2)

    def mid_last(rows):
        resid = [mid_resid(2, i) for i in rows]
        fresh = [mpre[i] + times(g, msmo[i]) for i, g in zip(rows, resid)]
        for i, z in zip(rows, fresh):
            v["mfield"][i] = z
            for h in range(HALVES):
                w["mround"][h][i] = z[h * rh : (h + 1) * rh].astype(BF16)

    for_rows(0, mcount, mid_last)

    def back_copy(h, k):
        return remote(
            w["backout"][h].at[k],
            w["backbox"][h].at[pl.ds(k * CAP, CAP)],
            q["back_send"].at[h, k],
            q["back_recv"].at[h, k],
            along_blk(k),
        )

    for h in range(HALVES):

        def wanted(k, s):
            place = goals[lax.rem(blks - k, blks), s, 0]
            return w["mround"][h][within(place, mcount)]

        def pack_back(k):
            for s in range(CAP):
                w["backout"][h][k, s] = wanted(k, s)
            back_copy(h, k).start()

        each(1, blks, pack_back)
        for s in range(CAP):
            w["backbox"][h][s] = wanted(0, s)
    keeps.append(pltpu.make_async_copy(v["mfield"], mid_o, q["keep"].at[1]))
    keeps[-1].start()

    for h in range(HALVES):
        each(1, blks, lambda k: back_copy(h, k).wait_recv())
        for part in range(PARTS):

            def fine_lift(rows):
                lifted = [
                    jnp.dot(
                        w["backbox"][h][within(v["places_s"][0, i], blks * CAP)],
                        chosen(slots, i),
                        preferred_element_type=F32,
                    )
                    for i in rows
                ]
                fresh = [pre[i, part_of_r(h), :] + z for i, z in zip(rows, lifted)]
                for i, z in zip(rows, fresh):
                    pre[i, part_of_r(h), :] = z
                    fine_wide(2, h)[count + i] = z.astype(BF16)

            for_rows(part * chunk, chunk, fine_lift)
            send(fine_halo(2, h, part))
    for h in range(HALVES):
        fine_own(2, h)
    for h in range(HALVES):
        fine_received(2, h)
        for part in range(PARTS):

            def fine_last(rows):
                resid = [fine_resid(2, h, i) for i in rows]
                fresh = [
                    pre[i, part_of_r(h), :] + times(g, smo[i])
                    for i, g in zip(rows, resid)
                ]
                for i, z in zip(rows, fresh):
                    pre[i, part_of_r(h), :] = z

            for_rows(part * chunk, chunk, fine_last)
            if h == HALVES - 1:
                rows = pl.ds(part * chunk, chunk)
                keeps.append(
                    pltpu.make_async_copy(
                        pre.at[rows], fine_o.at[rows], q["keep"].at[2 + part]
                    )
                )
                keeps[-1].start()

    for copy in sent:
        copy.wait_send()

    def end_sends(k):
        goal_copy(k).wait_send()
        for h in range(HALVES):
            piece_copy(h, k).wait_send()
            back_copy(h, k).wait_send()

    each(1, blks, end_sends)
    for copy in keeps:
        copy.wait()


def on_device(
    fine_rhs,
    fine_tiles,
    fine_cols,
    fine_smoother,
    fine_map,
    fine_slots,
    mid_tiles,
    mid_cols,
    mid_smoother,
    mid_map,
    mid_slots,
    coarse_tiles,
    coarse_cols,
    coarse_smoother,
):
    count, stored, width, _ = fine_tiles.shape
    mcount = mid_tiles.shape[0]
    lcount = coarse_tiles.shape[0]
    r = fine_rhs.shape[1]
    folds, blks = lax.axis_size("fold"), lax.axis_size("blk")
    half = lcount // 2
    rh, wide_r = r // HALVES, r * 2 // folds

    dma = pltpu.SemaphoreType.DMA

    def field(blocks, rows=r, kind=F32):
        return pltpu.VMEM((blocks, rows, width), kind)

    def tile(blocks, *more):
        return pltpu.VMEM((blocks, *more, width, width), BF16)

    arrays = {
        "tiles": tile(count, stored),
        "smo": tile(count),
        "rhs": field(count),
        "pre": field(count),
        "mtiles": tile(mcount, stored),
        "msmo": tile(mcount),
        "mrhs": field(mcount),
        "mpre": field(mcount),
        "mbase": field(mcount),
        "mpiece": field(mcount),
        "mfield": field(mcount),
        "ctiles": tile(half, stored),
        "csmo": tile(half),
        "crhs": field(half, wide_r),
        "cfield": field(half, wide_r),
        "cbase": field(half, wide_r),
        "fold_out": pltpu.VMEM((folds, half, wide_r, width), BF16),
        "fold_in": pltpu.VMEM((folds, half, wide_r, width), BF16),
        "gathered": pltpu.VMEM((folds, half, wide_r, width), BF16),
        "coarse": field(lcount),
        "fcols": pltpu.SMEM((stored, count), I32),
        "mcols": pltpu.SMEM((stored, mcount), I32),
        "ccols": pltpu.SMEM((stored, lcount), I32),
        "low": pltpu.SMEM((mcount,), I32),
        "fmap": pltpu.VMEM((1, count), I32),
        "slots": pltpu.VMEM((count, width), I32),
        "mslots": pltpu.VMEM((mcount, width), I32),
        "table": pltpu.VMEM((blks, SLOTS, 128), I32),
        "goals": pltpu.VMEM((blks, SLOTS, 128), I32),
        "places": pltpu.VMEM((SLOTS, 128), I32),
        "table_s": pltpu.SMEM((blks, SLOTS, 128), I32),
        "goals_s": pltpu.SMEM((blks, SLOTS, 128), I32),
        "places_s": pltpu.SMEM((SLOTS, 128), I32),
    }
    box = pltpu.VMEM((blks, CAP, rh, width), BF16)
    several = {
        "wide": [field(3 * count, rh, BF16)] * (3 * HALVES),
        "base": [field(count, rh)] * HALVES,
        "piece": [field(count, rh, BF16)] * HALVES,
        "outbox": [box] * HALVES,
        "inbox": [box] * HALVES,
        "backout": [box] * HALVES,
        "backbox": [field(blks * CAP, rh, BF16)] * HALVES,
        "mwide": [field(3 * mcount, r, BF16)] * 3,
        "mround": [field(mcount, rh, BF16)] * HALVES,
        "cwide": [field(3 * lcount, wide_r, BF16)] * COARSE,
    }
    sems = {
        "load": dma((2 * PARTS + 12,)),
        "small": dma((3,)),
        "keep": dma((2 + PARTS,)),
        "news": pltpu.SemaphoreType.REGULAR((8,)),
    }
    for name, shape in (
        ("halo", (3 * HALVES * PARTS, 2)),
        ("mid", (3, 2)),
        ("goal", (blks,)),
        ("piece", (HALVES, blks)),
        ("back", (HALVES, blks)),
        ("fold", (folds,)),
        ("gather", (folds,)),
        ("coarse", (COARSE - 1, 5 * SPLIT)),
    ):
        sems[name + "_send"] = dma(shape)
        sems[name + "_recv"] = dma(shape)

    hbm = pl.BlockSpec(memory_space=pltpu.HBM)
    anywhere = pl.BlockSpec(memory_space=pl.ANY)
    return pl.pallas_call(
        cycle,
        out_shape=(
            jax.ShapeDtypeStruct((count, r, width), F32),
            jax.ShapeDtypeStruct((mcount, r, width), F32),
            jax.ShapeDtypeStruct((lcount, r, width), F32),
        ),
        in_specs=[hbm] * 14,
        out_specs=(anywhere, anywhere, anywhere),
        scratch_shapes=[arrays, several, sems],
        compiler_params=pltpu.CompilerParams(
            collective_id=1, has_side_effects=True, vmem_limit_bytes=44 << 20
        ),
        name="cycle",
    )(
        fine_cols.T,
        mid_cols.T,
        coarse_cols.T,
        mid_map,
        fine_map.reshape(1, count),
        fine_slots,
        mid_slots,
        fine_rhs,
        fine_tiles,
        fine_smoother,
        mid_tiles,
        mid_smoother,
        coarse_tiles,
        coarse_smoother,
    )


def solution(mesh):
    both = ("fold", "blk")
    placed = (
        P(both, None, None),
        P(both, None, None, None),
        P(both, None),
        P(both, None, None),
        P(both),
        P(both, None),
        P(both, None, None, None),
        P(both, None),
        P(both, None, None),
        P(both),
        P(both, None),
        P("blk", None, None, None),
        P("blk", None),
        P("blk", None, None),
    )
    return jax.shard_map(
        on_device,
        mesh=mesh,
        in_specs=placed,
        out_specs=(P(both, None, None), P(both, None, None), P("blk", None, None)),
        check_vma=False,
    )
```

```python
import jax
import jax.numpy as jnp
from jax import lax
from jax.experimental import pallas as pl
from jax.experimental.pallas import tpu as pltpu
from jax.sharding import PartitionSpec as P

COARSE = 8
CAP = 3
HALVES = 2
PARTS = 2
SPLIT = 2
SLOTS = 8
MESH = pl.DeviceIdType.MESH
F32 = jnp.float32
BF16 = jnp.bfloat16
I32 = jnp.int32


def times(left, right):
    return lax.dot_general(
        left, right, (((1,), (1,)), ((), ())), preferred_element_type=F32
    )


def group_of(count, most):
    return max(size for size in range(1, most + 1) if count % size == 0)


def for_rows(start, count, body, most=12):
    size = group_of(count, most)

    def step(turn, carry):
        first = start + turn * size
        body([first + k for k in range(size)])
        return carry

    lax.fori_loop(0, count // size, step, 0)


def each(first, last, body):
    def step(k, carry):
        body(k)
        return carry

    lax.fori_loop(first, last, step, 0)


def chosen(slots, row):
    line = slots[pl.ds(row, 1), :]
    width = line.shape[1]
    places = lax.broadcasted_iota(I32, (width, width), 0)
    return jnp.where(places == line, 1.0, 0.0).astype(BF16)


def remote(source, target, send, recv, device):
    return pltpu.make_async_remote_copy(
        src_ref=source,
        dst_ref=target,
        send_sem=send,
        recv_sem=recv,
        device_id=device,
        device_id_type=MESH,
    )


def within(index, size):
    return jnp.minimum(jnp.maximum(index, 0), size - 1)


class Level:
    def __init__(self, tiles, cols, first, span, start=0):
        self.tiles, self.cols, self.start = tiles, cols, start
        self.first, self.span = first, span

    def own(self, row, value):
        return times(value, self.tiles[row, 0])

    def others(self, row, wide):
        stored = self.tiles.shape[1]
        picked = []
        for k in range(1, stored):
            at = self.cols[k, self.start + row] - self.first
            at = jnp.where(at < 0, at + self.span, at)
            at = jnp.where(at >= self.span, at - self.span, at)
            picked.append(wide[within(at, wide.shape[0])])
        tile = jnp.concatenate([self.tiles[row, k] for k in range(1, stored)], axis=1)
        return times(jnp.concatenate(picked, axis=1), tile)


def cycle(
    fcols_h,
    mcols_h,
    ccols_h,
    low_h,
    fmap_h,
    slots_h,
    mslots_h,
    rhs_h,
    tiles_h,
    smo_h,
    mtiles_h,
    msmo_h,
    ctiles_h,
    csmo_h,
    fine_o,
    mid_o,
    coarse_o,
    v,
    w,
    q,
):
    fold, blk = lax.axis_index("fold"), lax.axis_index("blk")
    folds, blks = lax.axis_size("fold"), lax.axis_size("blk")
    tiles, smo, rhs, pre = v["tiles"], v["smo"], v["rhs"], v["pre"]
    mtiles, msmo, mrhs, mpre = v["mtiles"], v["msmo"], v["mrhs"], v["mpre"]
    ctiles, csmo, crhs, cfield = v["ctiles"], v["csmo"], v["crhs"], v["cfield"]
    count, mcount, half = tiles.shape[0], mtiles.shape[0], ctiles.shape[0]
    rh = rhs.shape[1] // HALVES
    chunk = count // PARTS
    wide_r = crhs.shape[1]
    groups = folds // 2
    core = lax.rem(fold, 2)
    sent = []

    def along_blk(step):
        return (fold, lax.rem(blk + step + blks, blks))

    def along_fold(step):
        return (lax.rem(fold + step, folds), blk)

    def load(source, target, place, start=0, rows=None):
        if rows is not None:
            source, target = source.at[pl.ds(start, rows)], target.at[pl.ds(start, rows)]
        return pltpu.make_async_copy(source, target, q["load"].at[place])

    first_loads = []
    for part in range(PARTS):
        first_loads.append(load(rhs_h, rhs, 2 * part, part * chunk, chunk))
        first_loads.append(load(smo_h, smo, 2 * part + 1, part * chunk, chunk))
    tile_load = load(tiles_h, tiles, 2 * PARTS)
    later = [
        load(msmo_h, msmo, 2 * PARTS + 1),
        load(mtiles_h, mtiles, 2 * PARTS + 2),
        load(csmo_h.at[pl.ds(core * half, half)], csmo, 2 * PARTS + 3),
        load(ctiles_h.at[pl.ds(core * half, half)], ctiles, 2 * PARTS + 4),
    ]
    fcols, mcols, ccols, low = v["fcols"], v["mcols"], v["ccols"], v["low"]
    fmap, slots, mslots = v["fmap"], v["slots"], v["mslots"]
    table_loads = [
        load(source, target, 2 * PARTS + 5 + k)
        for k, (source, target) in enumerate(
            (
                (fmap_h, fmap),
                (fcols_h, fcols),
                (slots_h, slots),
                (mcols_h, mcols),
                (mslots_h, mslots),
                (low_h, low),
                (ccols_h, ccols),
            )
        )
    ]
    for copy in first_loads + table_loads[:3] + [tile_load]:
        copy.start()

    barrier = pltpu.get_barrier_semaphore()

    def greet(device):
        pl.semaphore_signal(barrier, inc=1, device_id=device, device_id_type=MESH)

    for step in (1, -1):
        greet(along_blk(step))
        greet(along_fold(step + folds))

    def spread(along, size, first):
        stages, reach = [], 1
        while 2 * reach < size:
            stages.append((along, reach, size, first + len(stages)))
            reach *= 2
        return stages

    blk_news = spread(along_blk, blks, 0)
    fold_news = spread(along_fold, folds, len(blk_news))
    turns = []
    for k in range(max(len(blk_news), len(fold_news)) + 1):
        turns.append([news[k : k + 1] for news in (blk_news, fold_news)])
    pending = []

    def next_stage():
        for place in pending:
            pl.semaphore_wait(q["news"].at[place], 2)
        pending.clear()
        if turns:
            for along, reach, size, place in sum(turns.pop(0), []):
                for step in (reach, size - reach):
                    pl.semaphore_signal(
                        q["news"].at[place],
                        inc=1,
                        device_id=along(step),
                        device_id_type=MESH,
                    )
                pending.append(place)

    fine = Level(tiles, fcols, (fold * blks + blk - 1) * count, blks * count)
    mid = Level(mtiles, mcols, (fold * blks + blk - 1) * mcount, blks * mcount)
    low_level = Level(
        ctiles, ccols, (blk - 1) * 2 * half, blks * 2 * half, core * half
    )

    def halo(wide, size, start, rows, sems, place):
        own = wide.at[pl.ds(size + start, rows)]
        return [
            remote(
                own,
                wide.at[pl.ds(at + start, rows)],
                q[sems + "_send"].at[place, side],
                q[sems + "_recv"].at[place, side],
                along_blk(step),
            )
            for side, (at, step) in enumerate(((0, 1), (2 * size, -1)))
        ]

    def send(copies):
        for copy in copies:
            copy.start()
        sent.extend(copies)

    def received(copies):
        for copy in copies:
            copy.wait_recv()

    def fine_halo(turn, h, part):
        place = (turn * HALVES + h) * PARTS + part
        return halo(w["wide"][turn * HALVES + h], count, part * chunk, chunk, "halo", place)

    def fine_wide(turn, h):
        return w["wide"][turn * HALVES + h]

    def fine_received(turn, h):
        for part in range(PARTS):
            received(fine_halo(turn, h, part))

    def part_of_r(h):
        return pl.ds(h * rh, rh)

    for part in range(PARTS):
        first_loads[2 * part].wait()
        first_loads[2 * part + 1].wait()

        def first_rows(rows):
            fresh = [times(rhs[i].astype(BF16), smo[i]) for i in rows]
            for i, z in zip(rows, fresh):
                pre[i] = z
                for h in range(HALVES):
                    fine_wide(0, h)[count + i] = z[h * rh : (h + 1) * rh].astype(BF16)

        for_rows(part * chunk, chunk, first_rows)
        if part == 0:
            pl.semaphore_wait(barrier, 4)
        send(fine_halo(0, 0, part))
    for h in range(1, HALVES):
        for part in range(PARTS):
            send(fine_halo(0, h, part))
    next_stage()
    for copy in later + table_loads[3:]:
        copy.start()
    for copy in table_loads[:3]:
        copy.wait()

    line = fmap[...] - fold * blks * mcount
    owner = lax.shift_right_logical(line * (-(-(1 << 19) // mcount)), 19)
    target = line - owner * mcount
    steps = owner - blk
    steps = jnp.where(steps < 0, steps + blks, steps)
    across = lax.broadcasted_iota(I32, (count, count), 1)
    down = lax.broadcasted_iota(I32, (count, count), 0)
    steps_down = jnp.sum(jnp.where(across == down, steps, 0), axis=1, keepdims=True)
    ahead = (steps_down == steps) & (down < across)
    rank = jnp.sum(jnp.where(ahead, 1, 0), axis=0, keepdims=True)
    position = steps * SLOTS + rank
    hit = lax.broadcasted_iota(I32, (blks * SLOTS, count), 0) == position
    order = lax.broadcasted_iota(I32, (blks * SLOTS, count), 1)
    index = jnp.sum(jnp.where(hit, order, 0), axis=1, keepdims=True)
    goal = jnp.sum(jnp.where(hit, target - mcount, 0), axis=1, keepdims=True) + mcount
    lane = lax.broadcasted_iota(I32, (blks * SLOTS, 128), 1)
    table = jnp.where(lane == 0, goal, index)
    v["table"][...] = table.reshape(blks, SLOTS, 128)
    back_steps = jnp.where(steps == 0, 0, blks - steps)
    v["places"][pl.ds(0, 1), pl.ds(0, count)] = back_steps * CAP + rank

    def small(source, target, place):
        return pltpu.make_async_copy(source, target, q["small"].at[place])

    own_table = small(v["table"], v["table_s"], 0)
    own_places = small(v["places"], v["places_s"], 1)
    own_table.start()
    own_places.start()

    def goal_copy(k):
        return remote(
            v["table"].at[k],
            v["goals"].at[k],
            q["goal_send"].at[k],
            q["goal_recv"].at[k],
            along_blk(k),
        )

    v["goals"][0] = v["table"][0]

    def fine_own(turn, h):
        def rows_of(rows):
            fresh = [
                rhs[i, part_of_r(h), :] - fine.own(i, fine_wide(turn, h)[count + i])
                for i in rows
            ]
            for i, z in zip(rows, fresh):
                w["base"][h][i] = z

        for_rows(0, count, rows_of)

    def fine_resid(turn, h, i):
        return (w["base"][h][i] - fine.others(i, fine_wide(turn, h))).astype(BF16)

    tile_load.wait()
    next_stage()
    for h in range(HALVES):
        fine_own(0, h)
        next_stage()

    for h in range(HALVES):
        fine_received(0, h)
        for part in range(PARTS):

            def sweep_rows(rows):
                resid = [fine_resid(0, h, i) for i in rows]
                fresh = [
                    pre[i, part_of_r(h), :] + times(g, smo[i])
                    for i, g in zip(rows, resid)
                ]
                for i, z in zip(rows, fresh):
                    pre[i, part_of_r(h), :] = z
                    fine_wide(1, h)[count + i] = z.astype(BF16)

            for_rows(part * chunk, chunk, sweep_rows)
            send(fine_halo(1, h, part))
        next_stage()
    while turns or pending:
        next_stage()
    each(1, blks, lambda k: goal_copy(k).start())
    for h in range(HALVES):
        fine_own(1, h)
    own_table.wait()
    own_places.wait()

    def piece_copy(h, k):
        return remote(
            w["outbox"][h].at[k],
            w["inbox"][h].at[k],
            q["piece_send"].at[h, k],
            q["piece_recv"].at[h, k],
            along_blk(k),
        )

    for h in range(HALVES):
        fine_received(1, h)
        piece = w["piece"][h]

        def piece_rows(rows):
            resid = [fine_resid(1, h, i) for i in rows]
            sums = [times(g, chosen(slots, i)) for i, g in zip(rows, resid)]
            for i, z in zip(rows, sums):
                piece[i] = z.astype(BF16)

        for_rows(0, count, piece_rows)

        def pack(k):
            for s in range(CAP):
                w["outbox"][h][k, s] = piece[within(v["table_s"][k, s, 1], count)]
            piece_copy(h, k).start()

        each(1, blks, pack)
        for s in range(CAP):
            w["inbox"][h][0, s] = piece[within(v["table_s"][0, s, 1], count)]

    each(1, blks, lambda k: goal_copy(k).wait_recv())
    goals_move = small(v["goals"], v["goals_s"], 2)
    goals_move.start()
    goals_move.wait()
    goals = v["goals_s"]

    zero = jnp.zeros((rh, rhs.shape[2]), F32)
    tied = group_of(mcount, 12)
    for h in range(HALVES):
        each(1, blks, lambda k: piece_copy(h, k).wait_recv())
        for first in range(0, mcount, tied):

            def add_pieces(k, sums):
                for s in range(CAP):
                    value = w["inbox"][h][k, s].astype(F32)
                    place = goals[k, s, 0]
                    sums = tuple(
                        total + jnp.where(place == first + t, value, zero)
                        for t, total in enumerate(sums)
                    )
                return sums

            sums = lax.fori_loop(0, blks, add_pieces, (zero,) * tied)
            for t, total in enumerate(sums):
                mrhs[first + t, part_of_r(h), :] = total
    for copy in later[:2] + table_loads[3:]:
        copy.wait()

    def mid_put(turn, rows, fresh):
        for i, z in zip(rows, fresh):
            mpre[i] = z
            w["mwide"][turn][mcount + i] = z.astype(BF16)

    def mid_first(rows):
        mid_put(0, rows, [times(mrhs[i].astype(BF16), msmo[i]) for i in rows])

    def mid_exchange(turn):
        wide = w["mwide"][turn]
        copies = halo(wide, mcount, 0, mcount, "mid", turn)
        send(copies)

        def own_rows(rows):
            fresh = [mrhs[i] - mid.own(i, wide[mcount + i]) for i in rows]
            for i, z in zip(rows, fresh):
                v["mbase"][i] = z

        for_rows(0, mcount, own_rows)
        received(copies)

    def mid_resid(turn, i):
        return (v["mbase"][i] - mid.others(i, w["mwide"][turn])).astype(BF16)

    for_rows(0, mcount, mid_first)
    mid_exchange(0)

    def mid_sweep(rows):
        resid = [mid_resid(0, i) for i in rows]
        mid_put(1, rows, [mpre[i] + times(g, msmo[i]) for i, g in zip(rows, resid)])

    for_rows(0, mcount, mid_sweep)
    mid_exchange(1)

    def mid_pieces(rows):
        resid = [mid_resid(1, i) for i in rows]
        sums = [times(g, chosen(mslots, i)) for i, g in zip(rows, resid)]
        for i, z in zip(rows, sums):
            v["mpiece"][i] = z

    for_rows(0, mcount, mid_pieces)

    whole_zero = jnp.zeros(mrhs.shape[1:], F32)
    low_first = blk * 2 * half

    def low_terms(c):
        total = whole_zero
        for j in range(mcount):
            total = total + jnp.where(low[j] - low_first == c, v["mpiece"][j], whole_zero)
        place = c // half
        row = lax.rem(c, half)
        for g in range(groups):
            v["fold_out"][2 * g + place, row] = total[
                g * wide_r : (g + 1) * wide_r
            ].astype(BF16)

    each(0, 2 * half, low_terms)

    fold_copies = [
        remote(
            v["fold_out"].at[along_fold(k)[0]],
            v["fold_in"].at[k],
            q["fold_send"].at[k],
            q["fold_recv"].at[k],
            along_fold(k),
        )
        for k in range(1, folds)
    ]
    send(fold_copies)
    v["fold_in"][0] = v["fold_out"][fold]
    for copy in later[2:]:
        copy.wait()
    received(fold_copies)
    total = v["fold_in"][0].astype(F32)
    for k in range(1, folds):
        total = total + v["fold_in"][k].astype(F32)
    crhs[...] = total

    mine = 2 * half + core * half
    other = fold + 1 - 2 * core
    piece_rows_c = half // group_of(half, SPLIT)

    def coarse_copies(turn):
        wide = w["cwide"][turn]
        copies = []
        place = 0
        for step, offset in ((1, 0), (-1, 2), (0, 1)):
            for device in (other,) if step == 0 else (fold, other):
                for part in range(half // piece_rows_c):
                    rows = part * piece_rows_c
                    copies.append(
                        remote(
                            wide.at[pl.ds(mine + rows, piece_rows_c)],
                            wide.at[
                                pl.ds(
                                    offset * 2 * half + core * half + rows, piece_rows_c
                                )
                            ],
                            q["coarse_send"].at[turn, place],
                            q["coarse_recv"].at[turn, place],
                            (device, lax.rem(blk + step + blks, blks)),
                        )
                    )
                    place += 1
        return copies

    def coarse_put(turn, rows, fresh):
        for i, z in zip(rows, fresh):
            cfield[i] = z
            w["cwide"][turn][mine + i] = z.astype(BF16)

    def coarse_first(rows):
        coarse_put(0, rows, [times(crhs[i].astype(BF16), csmo[i]) for i in rows])

    for_rows(0, half, coarse_first)
    for turn in range(COARSE - 1):
        wide = w["cwide"][turn]
        copies = coarse_copies(turn)
        send(copies)

        def coarse_own(rows):
            fresh = [crhs[i] - low_level.own(i, wide[mine + i]) for i in rows]
            for i, z in zip(rows, fresh):
                v["cbase"][i] = z

        for_rows(0, half, coarse_own)
        received(copies)

        def coarse_sweep(rows):
            resid = [
                (v["cbase"][i] - low_level.others(i, wide)).astype(BF16) for i in rows
            ]
            fresh = [cfield[i] + times(g, csmo[i]) for i, g in zip(rows, resid)]
            coarse_put(turn + 1, rows, fresh)

        for_rows(0, half, coarse_sweep)

    last_own = w["cwide"][COARSE - 1]
    gather_copies = [
        remote(
            last_own.at[pl.ds(mine, half)],
            v["gathered"].at[fold],
            q["gather_send"].at[k],
            q["gather_recv"].at[k],
            along_fold(k),
        )
        for k in range(1, folds)
    ]
    send(gather_copies)
    v["gathered"][fold] = last_own[pl.ds(mine, half)]
    received(gather_copies)
    for f in range(folds):
        g, place = f // 2, f % 2
        v["coarse"][pl.ds(place * half, half), pl.ds(g * wide_r, wide_r), :] = v[
            "gathered"
        ][f].astype(F32)
    keeps = [pltpu.make_async_copy(v["coarse"], coarse_o, q["keep"].at[0])]
    keeps[-1].start()

    def mid_lift(rows):
        lifted = [
            jnp.dot(
                v["coarse"][within(low[i] - low_first, 2 * half)].astype(BF16),
                chosen(mslots, i),
                preferred_element_type=F32,
            )
            for i in rows
        ]
        mid_put(2, rows, [mpre[i] + z for i, z in zip(rows, lifted)])

    for_rows(0, mcount, mid_lift)
    mid_exchange(2)

    def mid_last(rows):
        resid = [mid_resid(2, i) for i in rows]
        fresh = [mpre[i] + times(g, msmo[i]) for i, g in zip(rows, resid)]
        for i, z in zip(rows, fresh):
            v["mfield"][i] = z
            for h in range(HALVES):
                w["mround"][h][i] = z[h * rh : (h + 1) * rh].astype(BF16)

    for_rows(0, mcount, mid_last)

    def back_copy(h, k):
        return remote(
            w["backout"][h].at[k],
            w["backbox"][h].at[pl.ds(k * CAP, CAP)],
            q["back_send"].at[h, k],
            q["back_recv"].at[h, k],
            along_blk(k),
        )

    for h in range(HALVES):

        def wanted(k, s):
            place = goals[lax.rem(blks - k, blks), s, 0]
            return w["mround"][h][within(place, mcount)]

        def pack_back(k):
            for s in range(CAP):
                w["backout"][h][k, s] = wanted(k, s)
            back_copy(h, k).start()

        each(1, blks, pack_back)
        for s in range(CAP):
            w["backbox"][h][s] = wanted(0, s)
    keeps.append(pltpu.make_async_copy(v["mfield"], mid_o, q["keep"].at[1]))
    keeps[-1].start()

    for h in range(HALVES):
        each(1, blks, lambda k: back_copy(h, k).wait_recv())
        for part in range(PARTS):

            def fine_lift(rows):
                lifted = [
                    jnp.dot(
                        w["backbox"][h][within(v["places_s"][0, i], blks * CAP)],
                        chosen(slots, i),
                        preferred_element_type=F32,
                    )
                    for i in rows
                ]
                fresh = [pre[i, part_of_r(h), :] + z for i, z in zip(rows, lifted)]
                for i, z in zip(rows, fresh):
                    pre[i, part_of_r(h), :] = z
                    fine_wide(2, h)[count + i] = z.astype(BF16)

            for_rows(part * chunk, chunk, fine_lift)
            send(fine_halo(2, h, part))
    for h in range(HALVES):
        fine_own(2, h)
    for h in range(HALVES):
        fine_received(2, h)
        for part in range(PARTS):

            def fine_last(rows):
                resid = [fine_resid(2, h, i) for i in rows]
                fresh = [
                    pre[i, part_of_r(h), :] + times(g, smo[i])
                    for i, g in zip(rows, resid)
                ]
                for i, z in zip(rows, fresh):
                    pre[i, part_of_r(h), :] = z

            for_rows(part * chunk, chunk, fine_last)
            if h == HALVES - 1:
                rows = pl.ds(part * chunk, chunk)
                keeps.append(
                    pltpu.make_async_copy(
                        pre.at[rows], fine_o.at[rows], q["keep"].at[2 + part]
                    )
                )
                keeps[-1].start()

    for copy in sent:
        copy.wait_send()

    def end_sends(k):
        goal_copy(k).wait_send()
        for h in range(HALVES):
            piece_copy(h, k).wait_send()
            back_copy(h, k).wait_send()

    each(1, blks, end_sends)
    for copy in keeps:
        copy.wait()


def on_device(
    fine_rhs,
    fine_tiles,
    fine_cols,
    fine_smoother,
    fine_map,
    fine_slots,
    mid_tiles,
    mid_cols,
    mid_smoother,
    mid_map,
    mid_slots,
    coarse_tiles,
    coarse_cols,
    coarse_smoother,
):
    count, stored, width, _ = fine_tiles.shape
    mcount = mid_tiles.shape[0]
    lcount = coarse_tiles.shape[0]
    r = fine_rhs.shape[1]
    folds, blks = lax.axis_size("fold"), lax.axis_size("blk")
    half = lcount // 2
    rh, wide_r = r // HALVES, r * 2 // folds

    dma = pltpu.SemaphoreType.DMA

    def field(blocks, rows=r, kind=F32):
        return pltpu.VMEM((blocks, rows, width), kind)

    def tile(blocks, *more):
        return pltpu.VMEM((blocks, *more, width, width), BF16)

    arrays = {
        "tiles": tile(count, stored),
        "smo": tile(count),
        "rhs": field(count),
        "pre": field(count),
        "mtiles": tile(mcount, stored),
        "msmo": tile(mcount),
        "mrhs": field(mcount),
        "mpre": field(mcount),
        "mbase": field(mcount),
        "mpiece": field(mcount),
        "mfield": field(mcount),
        "ctiles": tile(half, stored),
        "csmo": tile(half),
        "crhs": field(half, wide_r),
        "cfield": field(half, wide_r),
        "cbase": field(half, wide_r),
        "fold_out": pltpu.VMEM((folds, half, wide_r, width), BF16),
        "fold_in": pltpu.VMEM((folds, half, wide_r, width), BF16),
        "gathered": pltpu.VMEM((folds, half, wide_r, width), BF16),
        "coarse": field(lcount),
        "fcols": pltpu.SMEM((stored, count), I32),
        "mcols": pltpu.SMEM((stored, mcount), I32),
        "ccols": pltpu.SMEM((stored, lcount), I32),
        "low": pltpu.SMEM((mcount,), I32),
        "fmap": pltpu.VMEM((1, count), I32),
        "slots": pltpu.VMEM((count, width), I32),
        "mslots": pltpu.VMEM((mcount, width), I32),
        "table": pltpu.VMEM((blks, SLOTS, 128), I32),
        "goals": pltpu.VMEM((blks, SLOTS, 128), I32),
        "places": pltpu.VMEM((SLOTS, 128), I32),
        "table_s": pltpu.SMEM((blks, SLOTS, 128), I32),
        "goals_s": pltpu.SMEM((blks, SLOTS, 128), I32),
        "places_s": pltpu.SMEM((SLOTS, 128), I32),
    }
    box = pltpu.VMEM((blks, CAP, rh, width), BF16)
    several = {
        "wide": [field(3 * count, rh, BF16)] * (3 * HALVES),
        "base": [field(count, rh)] * HALVES,
        "piece": [field(count, rh, BF16)] * HALVES,
        "outbox": [box] * HALVES,
        "inbox": [box] * HALVES,
        "backout": [box] * HALVES,
        "backbox": [field(blks * CAP, rh, BF16)] * HALVES,
        "mwide": [field(3 * mcount, r, BF16)] * 3,
        "mround": [field(mcount, rh, BF16)] * HALVES,
        "cwide": [field(3 * lcount, wide_r, BF16)] * COARSE,
    }
    sems = {
        "load": dma((2 * PARTS + 12,)),
        "small": dma((3,)),
        "keep": dma((2 + PARTS,)),
        "news": pltpu.SemaphoreType.REGULAR((8,)),
    }
    for name, shape in (
        ("halo", (3 * HALVES * PARTS, 2)),
        ("mid", (3, 2)),
        ("goal", (blks,)),
        ("piece", (HALVES, blks)),
        ("back", (HALVES, blks)),
        ("fold", (folds,)),
        ("gather", (folds,)),
        ("coarse", (COARSE - 1, 5 * SPLIT)),
    ):
        sems[name + "_send"] = dma(shape)
        sems[name + "_recv"] = dma(shape)

    hbm = pl.BlockSpec(memory_space=pltpu.HBM)
    anywhere = pl.BlockSpec(memory_space=pl.ANY)
    return pl.pallas_call(
        cycle,
        out_shape=(
            jax.ShapeDtypeStruct((count, r, width), F32),
            jax.ShapeDtypeStruct((mcount, r, width), F32),
            jax.ShapeDtypeStruct((lcount, r, width), F32),
        ),
        in_specs=[hbm] * 14,
        out_specs=(anywhere, anywhere, anywhere),
        scratch_shapes=[arrays, several, sems],
        compiler_params=pltpu.CompilerParams(
            collective_id=1, has_side_effects=True, vmem_limit_bytes=44 << 20
        ),
        name="cycle",
    )(
        *(
            pltpu.with_memory_space_constraint(value, pltpu.HBM)
            for value in (
                fine_cols.T,
                mid_cols.T,
                coarse_cols.T,
                mid_map,
                fine_map.reshape(1, count),
                fine_slots,
                mid_slots,
                fine_rhs,
                fine_tiles,
                fine_smoother,
                mid_tiles,
                mid_smoother,
                coarse_tiles,
                coarse_smoother,
            )
        )
    )


def solution(mesh):
    both = ("fold", "blk")
    placed = (
        P(both, None, None),
        P(both, None, None, None),
        P(both, None),
        P(both, None, None),
        P(both),
        P(both, None),
        P(both, None, None, None),
        P(both, None),
        P(both, None, None),
        P(both),
        P(both, None),
        P("blk", None, None, None),
        P("blk", None),
        P("blk", None, None),
    )
    return jax.shard_map(
        on_device,
        mesh=mesh,
        in_specs=placed,
        out_specs=(P(both, None, None), P(both, None, None), P("blk", None, None)),
        check_vma=False,
    )
```

```python
import jax
import jax.numpy as jnp
from jax import lax
from jax.experimental import pallas as pl
from jax.experimental.pallas import tpu as pltpu
from jax.sharding import PartitionSpec as P

COARSE = 8
CAP = 3
HALVES = 2
PARTS = 2
SPLIT = 2
SLOTS = 8
MESH = pl.DeviceIdType.MESH
F32 = jnp.float32
BF16 = jnp.bfloat16
I32 = jnp.int32


def times(left, right):
    return lax.dot_general(
        left, right, (((1,), (1,)), ((), ())), preferred_element_type=F32
    )


def group_of(count, most):
    return max(size for size in range(1, most + 1) if count % size == 0)


def for_rows(start, count, body, most=24):
    size = group_of(count, most)

    def step(turn, carry):
        first = start + turn * size
        body([first + k for k in range(size)])
        return carry

    lax.fori_loop(0, count // size, step, 0)


def each(first, last, body):
    def step(k, carry):
        body(k)
        return carry

    lax.fori_loop(first, last, step, 0)


def chosen(slots, row):
    line = slots[pl.ds(row, 1), :]
    width = line.shape[1]
    places = lax.broadcasted_iota(I32, (width, width), 0)
    return jnp.where(places == line, 1.0, 0.0).astype(BF16)


def remote(source, target, send, recv, device):
    return pltpu.make_async_remote_copy(
        src_ref=source,
        dst_ref=target,
        send_sem=send,
        recv_sem=recv,
        device_id=device,
        device_id_type=MESH,
    )


def within(index, size):
    return jnp.minimum(jnp.maximum(index, 0), size - 1)


class Level:
    def __init__(self, tiles, cols, first, span, start=0):
        self.tiles, self.cols, self.start = tiles, cols, start
        self.first, self.span = first, span

    def own(self, row, value):
        return times(value, self.tiles[row, 0])

    def others(self, row, wide):
        stored = self.tiles.shape[1]
        picked = []
        for k in range(1, stored):
            at = self.cols[k, self.start + row] - self.first
            at = jnp.where(at < 0, at + self.span, at)
            at = jnp.where(at >= self.span, at - self.span, at)
            picked.append(wide[within(at, wide.shape[0])])
        tile = jnp.concatenate([self.tiles[row, k] for k in range(1, stored)], axis=1)
        return times(jnp.concatenate(picked, axis=1), tile)


def cycle(
    fcols_h,
    mcols_h,
    ccols_h,
    low_h,
    fmap_h,
    slots_h,
    mslots_h,
    rhs_h,
    tiles_h,
    smo_h,
    mtiles_h,
    msmo_h,
    ctiles_h,
    csmo_h,
    fine_o,
    mid_o,
    coarse_o,
    v,
    w,
    q,
):
    fold, blk = lax.axis_index("fold"), lax.axis_index("blk")
    folds, blks = lax.axis_size("fold"), lax.axis_size("blk")
    tiles, smo, rhs, pre = v["tiles"], v["smo"], v["rhs"], v["pre"]
    mtiles, msmo, mrhs, mpre = v["mtiles"], v["msmo"], v["mrhs"], v["mpre"]
    ctiles, csmo, crhs, cfield = v["ctiles"], v["csmo"], v["crhs"], v["cfield"]
    count, mcount, half = tiles.shape[0], mtiles.shape[0], ctiles.shape[0]
    rh = rhs.shape[1] // HALVES
    chunk = count // PARTS
    wide_r = crhs.shape[1]
    groups = folds // 2
    core = lax.rem(fold, 2)
    sent = []

    def along_blk(step):
        return (fold, lax.rem(blk + step + blks, blks))

    def along_fold(step):
        return (lax.rem(fold + step, folds), blk)

    def load(source, target, place, start=0, rows=None):
        if rows is not None:
            source, target = source.at[pl.ds(start, rows)], target.at[pl.ds(start, rows)]
        return pltpu.make_async_copy(source, target, q["load"].at[place])

    first_loads = []
    for part in range(PARTS):
        first_loads.append(load(rhs_h, rhs, 2 * part, part * chunk, chunk))
        first_loads.append(load(smo_h, smo, 2 * part + 1, part * chunk, chunk))
    tile_load = load(tiles_h, tiles, 2 * PARTS)
    later = [
        load(msmo_h, msmo, 2 * PARTS + 1),
        load(mtiles_h, mtiles, 2 * PARTS + 2),
        load(csmo_h.at[pl.ds(core * half, half)], csmo, 2 * PARTS + 3),
        load(ctiles_h.at[pl.ds(core * half, half)], ctiles, 2 * PARTS + 4),
    ]
    fcols, mcols, ccols, low = v["fcols"], v["mcols"], v["ccols"], v["low"]
    fmap, slots, mslots = v["fmap"], v["slots"], v["mslots"]
    table_loads = [
        load(source, target, 2 * PARTS + 5 + k)
        for k, (source, target) in enumerate(
            (
                (fmap_h, fmap),
                (fcols_h, fcols),
                (slots_h, slots),
                (mcols_h, mcols),
                (mslots_h, mslots),
                (low_h, low),
                (ccols_h, ccols),
            )
        )
    ]
    for copy in first_loads + table_loads[:3] + [tile_load]:
        copy.start()

    barrier = pltpu.get_barrier_semaphore()

    def greet(device):
        pl.semaphore_signal(barrier, inc=1, device_id=device, device_id_type=MESH)

    for step in (1, -1):
        greet(along_blk(step))
        greet(along_fold(step + folds))

    def spread(along, size, first):
        stages, reach = [], 1
        while 2 * reach < size:
            stages.append((along, reach, size, first + len(stages)))
            reach *= 2
        return stages

    blk_news = spread(along_blk, blks, 0)
    fold_news = spread(along_fold, folds, len(blk_news))
    turns = []
    for k in range(max(len(blk_news), len(fold_news)) + 1):
        turns.append([news[k : k + 1] for news in (blk_news, fold_news)])
    pending = []

    def next_stage():
        for place in pending:
            pl.semaphore_wait(q["news"].at[place], 2)
        pending.clear()
        if turns:
            for along, reach, size, place in sum(turns.pop(0), []):
                for step in (reach, size - reach):
                    pl.semaphore_signal(
                        q["news"].at[place],
                        inc=1,
                        device_id=along(step),
                        device_id_type=MESH,
                    )
                pending.append(place)

    fine = Level(tiles, fcols, (fold * blks + blk - 1) * count, blks * count)
    mid = Level(mtiles, mcols, (fold * blks + blk - 1) * mcount, blks * mcount)
    low_level = Level(
        ctiles, ccols, (blk - 1) * 2 * half, blks * 2 * half, core * half
    )

    def halo(wide, size, start, rows, sems, place):
        own = wide.at[pl.ds(size + start, rows)]
        return [
            remote(
                own,
                wide.at[pl.ds(at + start, rows)],
                q[sems + "_send"].at[place, side],
                q[sems + "_recv"].at[place, side],
                along_blk(step),
            )
            for side, (at, step) in enumerate(((0, 1), (2 * size, -1)))
        ]

    def send(copies):
        for copy in copies:
            copy.start()
        sent.extend(copies)

    def received(copies):
        for copy in copies:
            copy.wait_recv()

    def fine_halo(turn, h, part):
        place = (turn * HALVES + h) * PARTS + part
        return halo(w["wide"][turn * HALVES + h], count, part * chunk, chunk, "halo", place)

    def fine_wide(turn, h):
        return w["wide"][turn * HALVES + h]

    def fine_received(turn, h):
        for part in range(PARTS):
            received(fine_halo(turn, h, part))

    def part_of_r(h):
        return pl.ds(h * rh, rh)

    for part in range(PARTS):
        first_loads[2 * part].wait()
        first_loads[2 * part + 1].wait()

        def first_rows(rows):
            fresh = [times(rhs[i].astype(BF16), smo[i]) for i in rows]
            for i, z in zip(rows, fresh):
                pre[i] = z
                for h in range(HALVES):
                    fine_wide(0, h)[count + i] = z[h * rh : (h + 1) * rh].astype(BF16)

        for_rows(part * chunk, chunk, first_rows)
        if part == 0:
            pl.semaphore_wait(barrier, 4)
        send(fine_halo(0, 0, part))
    for h in range(1, HALVES):
        for part in range(PARTS):
            send(fine_halo(0, h, part))
    next_stage()
    for copy in later + table_loads[3:]:
        copy.start()
    for copy in table_loads[:3]:
        copy.wait()

    line = fmap[...] - fold * blks * mcount
    owner = lax.shift_right_logical(line * (-(-(1 << 19) // mcount)), 19)
    target = line - owner * mcount
    steps = owner - blk
    steps = jnp.where(steps < 0, steps + blks, steps)
    across = lax.broadcasted_iota(I32, (count, count), 1)
    down = lax.broadcasted_iota(I32, (count, count), 0)
    steps_down = jnp.sum(jnp.where(across == down, steps, 0), axis=1, keepdims=True)
    ahead = (steps_down == steps) & (down < across)
    rank = jnp.sum(jnp.where(ahead, 1, 0), axis=0, keepdims=True)
    position = steps * SLOTS + rank
    hit = lax.broadcasted_iota(I32, (blks * SLOTS, count), 0) == position
    order = lax.broadcasted_iota(I32, (blks * SLOTS, count), 1)
    index = jnp.sum(jnp.where(hit, order, 0), axis=1, keepdims=True)
    goal = jnp.sum(jnp.where(hit, target - mcount, 0), axis=1, keepdims=True) + mcount
    lane = lax.broadcasted_iota(I32, (blks * SLOTS, 128), 1)
    table = jnp.where(lane == 0, goal, index)
    v["table"][...] = table.reshape(blks, SLOTS, 128)
    back_steps = jnp.where(steps == 0, 0, blks - steps)
    v["places"][pl.ds(0, 1), pl.ds(0, count)] = back_steps * CAP + rank

    def small(source, target, place):
        return pltpu.make_async_copy(source, target, q["small"].at[place])

    own_table = small(v["table"], v["table_s"], 0)
    own_places = small(v["places"], v["places_s"], 1)
    own_table.start()
    own_places.start()

    def goal_copy(k):
        return remote(
            v["table"].at[k],
            v["goals"].at[k],
            q["goal_send"].at[k],
            q["goal_recv"].at[k],
            along_blk(k),
        )

    v["goals"][0] = v["table"][0]

    def fine_own(turn, h):
        def rows_of(rows):
            fresh = [
                rhs[i, part_of_r(h), :] - fine.own(i, fine_wide(turn, h)[count + i])
                for i in rows
            ]
            for i, z in zip(rows, fresh):
                w["base"][h][i] = z

        for_rows(0, count, rows_of)

    def fine_resid(turn, h, i):
        return (w["base"][h][i] - fine.others(i, fine_wide(turn, h))).astype(BF16)

    tile_load.wait()
    next_stage()
    for h in range(HALVES):
        fine_own(0, h)
        next_stage()

    for h in range(HALVES):
        fine_received(0, h)
        for part in range(PARTS):

            def sweep_rows(rows):
                resid = [fine_resid(0, h, i) for i in rows]
                fresh = [
                    pre[i, part_of_r(h), :] + times(g, smo[i])
                    for i, g in zip(rows, resid)
                ]
                for i, z in zip(rows, fresh):
                    pre[i, part_of_r(h), :] = z
                    fine_wide(1, h)[count + i] = z.astype(BF16)

            for_rows(part * chunk, chunk, sweep_rows)
            send(fine_halo(1, h, part))
        next_stage()
    while turns or pending:
        next_stage()
    fine_own(1, 0)
    own_table.wait()
    own_places.wait()

    def piece_copy(h, k):
        return remote(
            w["outbox"][h].at[k],
            w["inbox"][h].at[k],
            q["piece_send"].at[h, k],
            q["piece_recv"].at[h, k],
            along_blk(k),
        )

    for h in range(HALVES):
        fine_received(1, h)
        piece = w["piece"][h]

        def piece_rows(rows):
            resid = [fine_resid(1, h, i) for i in rows]
            sums = [times(g, chosen(slots, i)) for i, g in zip(rows, resid)]
            for i, z in zip(rows, sums):
                piece[i] = z.astype(BF16)

        for_rows(0, count, piece_rows)

        def pack(k):
            for s in range(CAP):
                w["outbox"][h][k, s] = piece[within(v["table_s"][k, s, 1], count)]
            piece_copy(h, k).start()

        each(1, blks, pack)
        for s in range(CAP):
            w["inbox"][h][0, s] = piece[within(v["table_s"][0, s, 1], count)]
        if h == 0:
            each(1, blks, lambda k: goal_copy(k).start())
        if h + 1 < HALVES:
            fine_own(1, h + 1)

    each(1, blks, lambda k: goal_copy(k).wait_recv())
    goals_move = small(v["goals"], v["goals_s"], 2)
    goals_move.start()
    goals_move.wait()
    goals = v["goals_s"]

    zero = jnp.zeros((rh, rhs.shape[2]), F32)
    tied = group_of(mcount, 12)
    for h in range(HALVES):
        each(1, blks, lambda k: piece_copy(h, k).wait_recv())
        for first in range(0, mcount, tied):

            def add_pieces(k, sums):
                for s in range(CAP):
                    value = w["inbox"][h][k, s].astype(F32)
                    place = goals[k, s, 0]
                    sums = tuple(
                        total + jnp.where(place == first + t, value, zero)
                        for t, total in enumerate(sums)
                    )
                return sums

            sums = lax.fori_loop(0, blks, add_pieces, (zero,) * tied)
            for t, total in enumerate(sums):
                mrhs[first + t, part_of_r(h), :] = total
    for copy in later[:2] + table_loads[3:]:
        copy.wait()

    def mid_put(turn, rows, fresh):
        for i, z in zip(rows, fresh):
            mpre[i] = z
            w["mwide"][turn][mcount + i] = z.astype(BF16)

    def mid_first(rows):
        mid_put(0, rows, [times(mrhs[i].astype(BF16), msmo[i]) for i in rows])

    def mid_exchange(turn):
        wide = w["mwide"][turn]
        copies = halo(wide, mcount, 0, mcount, "mid", turn)
        send(copies)

        def own_rows(rows):
            fresh = [mrhs[i] - mid.own(i, wide[mcount + i]) for i in rows]
            for i, z in zip(rows, fresh):
                v["mbase"][i] = z

        for_rows(0, mcount, own_rows)
        received(copies)

    def mid_resid(turn, i):
        return (v["mbase"][i] - mid.others(i, w["mwide"][turn])).astype(BF16)

    for_rows(0, mcount, mid_first)
    mid_exchange(0)

    def mid_sweep(rows):
        resid = [mid_resid(0, i) for i in rows]
        mid_put(1, rows, [mpre[i] + times(g, msmo[i]) for i, g in zip(rows, resid)])

    for_rows(0, mcount, mid_sweep)
    mid_exchange(1)

    def mid_pieces(rows):
        resid = [mid_resid(1, i) for i in rows]
        sums = [times(g, chosen(mslots, i)) for i, g in zip(rows, resid)]
        for i, z in zip(rows, sums):
            v["mpiece"][i] = z

    for_rows(0, mcount, mid_pieces)

    whole_zero = jnp.zeros(mrhs.shape[1:], F32)
    low_first = blk * 2 * half

    def low_terms(c):
        total = whole_zero
        for j in range(mcount):
            total = total + jnp.where(low[j] - low_first == c, v["mpiece"][j], whole_zero)
        place = c // half
        row = lax.rem(c, half)
        for g in range(groups):
            v["fold_out"][2 * g + place, row] = total[
                g * wide_r : (g + 1) * wide_r
            ].astype(BF16)

    each(0, 2 * half, low_terms)

    fold_copies = [
        remote(
            v["fold_out"].at[along_fold(k)[0]],
            v["fold_in"].at[k],
            q["fold_send"].at[k],
            q["fold_recv"].at[k],
            along_fold(k),
        )
        for k in range(1, folds)
    ]
    send(fold_copies)
    v["fold_in"][0] = v["fold_out"][fold]
    for copy in later[2:]:
        copy.wait()
    received(fold_copies)
    total = v["fold_in"][0].astype(F32)
    for k in range(1, folds):
        total = total + v["fold_in"][k].astype(F32)
    crhs[...] = total

    mine = 2 * half + core * half
    other = fold + 1 - 2 * core
    piece_rows_c = half // group_of(half, SPLIT)

    def coarse_copies(turn):
        wide = w["cwide"][turn]
        copies = []
        place = 0
        for step, offset in ((1, 0), (-1, 2), (0, 1)):
            for device in (other,) if step == 0 else (fold, other):
                for part in range(half // piece_rows_c):
                    rows = part * piece_rows_c
                    copies.append(
                        remote(
                            wide.at[pl.ds(mine + rows, piece_rows_c)],
                            wide.at[
                                pl.ds(
                                    offset * 2 * half + core * half + rows, piece_rows_c
                                )
                            ],
                            q["coarse_send"].at[turn, place],
                            q["coarse_recv"].at[turn, place],
                            (device, lax.rem(blk + step + blks, blks)),
                        )
                    )
                    place += 1
        return copies

    def coarse_put(turn, rows, fresh):
        for i, z in zip(rows, fresh):
            cfield[i] = z
            w["cwide"][turn][mine + i] = z.astype(BF16)

    def coarse_first(rows):
        coarse_put(0, rows, [times(crhs[i].astype(BF16), csmo[i]) for i in rows])

    for_rows(0, half, coarse_first)
    for turn in range(COARSE - 1):
        wide = w["cwide"][turn]
        copies = coarse_copies(turn)
        send(copies)

        def coarse_own(rows):
            fresh = [crhs[i] - low_level.own(i, wide[mine + i]) for i in rows]
            for i, z in zip(rows, fresh):
                v["cbase"][i] = z

        for_rows(0, half, coarse_own)
        received(copies)

        def coarse_sweep(rows):
            resid = [
                (v["cbase"][i] - low_level.others(i, wide)).astype(BF16) for i in rows
            ]
            fresh = [cfield[i] + times(g, csmo[i]) for i, g in zip(rows, resid)]
            coarse_put(turn + 1, rows, fresh)

        for_rows(0, half, coarse_sweep)

    last_own = w["cwide"][COARSE - 1]
    gather_copies = [
        remote(
            last_own.at[pl.ds(mine, half)],
            v["gathered"].at[fold],
            q["gather_send"].at[k],
            q["gather_recv"].at[k],
            along_fold(k),
        )
        for k in range(1, folds)
    ]
    send(gather_copies)
    v["gathered"][fold] = last_own[pl.ds(mine, half)]
    received(gather_copies)
    for f in range(folds):
        g, place = f // 2, f % 2
        v["coarse"][pl.ds(place * half, half), pl.ds(g * wide_r, wide_r), :] = v[
            "gathered"
        ][f].astype(F32)
    keeps = [pltpu.make_async_copy(v["coarse"], coarse_o, q["keep"].at[0])]
    keeps[-1].start()

    def mid_lift(rows):
        lifted = [
            jnp.dot(
                v["coarse"][within(low[i] - low_first, 2 * half)].astype(BF16),
                chosen(mslots, i),
                preferred_element_type=F32,
            )
            for i in rows
        ]
        mid_put(2, rows, [mpre[i] + z for i, z in zip(rows, lifted)])

    for_rows(0, mcount, mid_lift)
    mid_exchange(2)

    def mid_last(rows):
        resid = [mid_resid(2, i) for i in rows]
        fresh = [mpre[i] + times(g, msmo[i]) for i, g in zip(rows, resid)]
        for i, z in zip(rows, fresh):
            v["mfield"][i] = z
            for h in range(HALVES):
                w["mround"][h][i] = z[h * rh : (h + 1) * rh].astype(BF16)

    for_rows(0, mcount, mid_last)

    def back_copy(h, k):
        return remote(
            w["backout"][h].at[k],
            w["backbox"][h].at[pl.ds(k * CAP, CAP)],
            q["back_send"].at[h, k],
            q["back_recv"].at[h, k],
            along_blk(k),
        )

    for h in range(HALVES):

        def wanted(k, s):
            place = goals[lax.rem(blks - k, blks), s, 0]
            return w["mround"][h][within(place, mcount)]

        def pack_back(k):
            for s in range(CAP):
                w["backout"][h][k, s] = wanted(k, s)
            back_copy(h, k).start()

        each(1, blks, pack_back)
        for s in range(CAP):
            w["backbox"][h][s] = wanted(0, s)
    keeps.append(pltpu.make_async_copy(v["mfield"], mid_o, q["keep"].at[1]))
    keeps[-1].start()

    for h in range(HALVES):
        each(1, blks, lambda k: back_copy(h, k).wait_recv())
        for part in range(PARTS):

            def fine_lift(rows):
                lifted = [
                    jnp.dot(
                        w["backbox"][h][within(v["places_s"][0, i], blks * CAP)],
                        chosen(slots, i),
                        preferred_element_type=F32,
                    )
                    for i in rows
                ]
                fresh = [pre[i, part_of_r(h), :] + z for i, z in zip(rows, lifted)]
                for i, z in zip(rows, fresh):
                    pre[i, part_of_r(h), :] = z
                    fine_wide(2, h)[count + i] = z.astype(BF16)

            for_rows(part * chunk, chunk, fine_lift)
            send(fine_halo(2, h, part))
    for h in range(HALVES):
        fine_own(2, h)
    for h in range(HALVES):
        fine_received(2, h)
        for part in range(PARTS):

            def fine_last(rows):
                resid = [fine_resid(2, h, i) for i in rows]
                fresh = [
                    pre[i, part_of_r(h), :] + times(g, smo[i])
                    for i, g in zip(rows, resid)
                ]
                for i, z in zip(rows, fresh):
                    pre[i, part_of_r(h), :] = z

            for_rows(part * chunk, chunk, fine_last)
            if h == HALVES - 1:
                rows = pl.ds(part * chunk, chunk)
                keeps.append(
                    pltpu.make_async_copy(
                        pre.at[rows], fine_o.at[rows], q["keep"].at[2 + part]
                    )
                )
                keeps[-1].start()

    for copy in sent:
        copy.wait_send()

    def end_sends(k):
        goal_copy(k).wait_send()
        for h in range(HALVES):
            piece_copy(h, k).wait_send()
            back_copy(h, k).wait_send()

    each(1, blks, end_sends)
    for copy in keeps:
        copy.wait()


def on_device(
    fine_rhs,
    fine_tiles,
    fine_cols,
    fine_smoother,
    fine_map,
    fine_slots,
    mid_tiles,
    mid_cols,
    mid_smoother,
    mid_map,
    mid_slots,
    coarse_tiles,
    coarse_cols,
    coarse_smoother,
):
    count, stored, width, _ = fine_tiles.shape
    mcount = mid_tiles.shape[0]
    lcount = coarse_tiles.shape[0]
    r = fine_rhs.shape[1]
    folds, blks = lax.axis_size("fold"), lax.axis_size("blk")
    half = lcount // 2
    rh, wide_r = r // HALVES, r * 2 // folds

    dma = pltpu.SemaphoreType.DMA

    def field(blocks, rows=r, kind=F32):
        return pltpu.VMEM((blocks, rows, width), kind)

    def tile(blocks, *more):
        return pltpu.VMEM((blocks, *more, width, width), BF16)

    arrays = {
        "tiles": tile(count, stored),
        "smo": tile(count),
        "rhs": field(count),
        "pre": field(count),
        "mtiles": tile(mcount, stored),
        "msmo": tile(mcount),
        "mrhs": field(mcount),
        "mpre": field(mcount),
        "mbase": field(mcount),
        "mpiece": field(mcount),
        "mfield": field(mcount),
        "ctiles": tile(half, stored),
        "csmo": tile(half),
        "crhs": field(half, wide_r),
        "cfield": field(half, wide_r),
        "cbase": field(half, wide_r),
        "fold_out": pltpu.VMEM((folds, half, wide_r, width), BF16),
        "fold_in": pltpu.VMEM((folds, half, wide_r, width), BF16),
        "gathered": pltpu.VMEM((folds, half, wide_r, width), BF16),
        "coarse": field(lcount),
        "fcols": pltpu.SMEM((stored, count), I32),
        "mcols": pltpu.SMEM((stored, mcount), I32),
        "ccols": pltpu.SMEM((stored, lcount), I32),
        "low": pltpu.SMEM((mcount,), I32),
        "fmap": pltpu.VMEM((1, count), I32),
        "slots": pltpu.VMEM((count, width), I32),
        "mslots": pltpu.VMEM((mcount, width), I32),
        "table": pltpu.VMEM((blks, SLOTS, 128), I32),
        "goals": pltpu.VMEM((blks, SLOTS, 128), I32),
        "places": pltpu.VMEM((SLOTS, 128), I32),
        "table_s": pltpu.SMEM((blks, SLOTS, 128), I32),
        "goals_s": pltpu.SMEM((blks, SLOTS, 128), I32),
        "places_s": pltpu.SMEM((SLOTS, 128), I32),
    }
    box = pltpu.VMEM((blks, CAP, rh, width), BF16)
    several = {
        "wide": [field(3 * count, rh, BF16)] * (3 * HALVES),
        "base": [field(count, rh)] * HALVES,
        "piece": [field(count, rh, BF16)] * HALVES,
        "outbox": [box] * HALVES,
        "inbox": [box] * HALVES,
        "backout": [box] * HALVES,
        "backbox": [field(blks * CAP, rh, BF16)] * HALVES,
        "mwide": [field(3 * mcount, r, BF16)] * 3,
        "mround": [field(mcount, rh, BF16)] * HALVES,
        "cwide": [field(3 * lcount, wide_r, BF16)] * COARSE,
    }
    sems = {
        "load": dma((2 * PARTS + 12,)),
        "small": dma((3,)),
        "keep": dma((2 + PARTS,)),
        "news": pltpu.SemaphoreType.REGULAR((8,)),
    }
    for name, shape in (
        ("halo", (3 * HALVES * PARTS, 2)),
        ("mid", (3, 2)),
        ("goal", (blks,)),
        ("piece", (HALVES, blks)),
        ("back", (HALVES, blks)),
        ("fold", (folds,)),
        ("gather", (folds,)),
        ("coarse", (COARSE - 1, 5 * SPLIT)),
    ):
        sems[name + "_send"] = dma(shape)
        sems[name + "_recv"] = dma(shape)

    hbm = pl.BlockSpec(memory_space=pltpu.HBM)
    anywhere = pl.BlockSpec(memory_space=pl.ANY)
    return pl.pallas_call(
        cycle,
        out_shape=(
            jax.ShapeDtypeStruct((count, r, width), F32),
            jax.ShapeDtypeStruct((mcount, r, width), F32),
            jax.ShapeDtypeStruct((lcount, r, width), F32),
        ),
        in_specs=[hbm] * 14,
        out_specs=(anywhere, anywhere, anywhere),
        scratch_shapes=[arrays, several, sems],
        compiler_params=pltpu.CompilerParams(
            collective_id=1, has_side_effects=True, vmem_limit_bytes=44 << 20
        ),
        name="cycle",
    )(
        *(
            pltpu.with_memory_space_constraint(value, pltpu.HBM)
            for value in (
                fine_cols.T,
                mid_cols.T,
                coarse_cols.T,
                mid_map,
                fine_map.reshape(1, count),
                fine_slots,
                mid_slots,
                fine_rhs,
                fine_tiles,
                fine_smoother,
                mid_tiles,
                mid_smoother,
                coarse_tiles,
                coarse_smoother,
            )
        )
    )


def solution(mesh):
    both = ("fold", "blk")
    placed = (
        P(both, None, None),
        P(both, None, None, None),
        P(both, None),
        P(both, None, None),
        P(both),
        P(both, None),
        P(both, None, None, None),
        P(both, None),
        P(both, None, None),
        P(both),
        P(both, None),
        P("blk", None, None, None),
        P("blk", None),
        P("blk", None, None),
    )
    return jax.shard_map(
        on_device,
        mesh=mesh,
        in_specs=placed,
        out_specs=(P(both, None, None), P(both, None, None), P("blk", None, None)),
        check_vma=False,
    )
```
